128 devices in a mesh: dir: 2 (over z_lo), row: 8 (over y, z_hi), col: 8 (over x, core).
Axes of the slice: x: 4, y: 4, z: 4 (z_hi: 2, z_lo: 2; z = z_hi * 2 + z_lo), core: 2. Of those that a mesh axis runs over, the one named last changes fastest.
Arguments:
- cotangent: bfloat16 [2048, 512], P('dir'), may hold values from -3 to 3
- radiation: bfloat16 [2, 32768, 2048], P(None, ('row', 'col'), 'dir'), may hold values from -0.125 to 0.125
- near_z: float32 [2, 1024, 512, 512], P(None, ('dir', 'row', 'col')), may hold values from -0.25 to 0.25
- near_pairs: int32 [1024, 2], P(('dir', 'row', 'col')), may hold values from 0 to 63, as said below
- far_ut: float32 [2, 512, 96, 512], P(None, ('dir', 'row', 'col')), may hold values from -0.25 to 0.25
- far_vt: float32 [2, 512, 96, 512], P(None, ('dir', 'row', 'col')), may hold values from -0.625 to 0.625
- far_pairs: int32 [512, 2], P(('dir', 'row', 'col')), may hold values from 0 to 63, as said below
- far_ranks: int32 [512], P(('dir', 'row', 'col')), may hold values from 32 to 96
- block_counts: int32 [128, 2], P(('dir', 'row', 'col')), may hold values from 1 to 8, as said below
Outputs:
- adjoint: float32 [32768, 512], P(('col', 'dir', 'row'))
The draws below stay inside these ranges and needn't reach their ends.
Inputs may be any that keep to these rules, and one draw needn't show every extreme that they name: `near_pairs`: slot s belongs to the device at position g = s div 8 in the order dir, row, col, with row index r and column index c; its row cluster lies in r * 8 to (r + 1) * 8 - 1 and its column cluster in c * 8 to (c + 1) * 8 - 1. Pairs may repeat. `far_pairs`: slot s belongs to the device at position s div 4 in the order dir, row, col, with row index r and column index c; its row cluster lies in r * 8 to (r + 1) * 8 - 1 and its column cluster in c * 8 to (c + 1) * 8 - 1. Pairs may repeat. `block_counts`: column 0 is at most 8 and column 1 at most 4; the live slots of a device are its first ones.
All inputs are finite; a program needn't handle non-finite values.
Results may differ from the reference program's by a relative error of at most 0.0003.
Values sent between devices are 32-bit elements; how exact they have to be, the bound alone decides.
No kernel may reach another device: no remote copies, remote signals or barrier semaphores. Data moves between devices by JAX's collectives and lax.ppermute only.
A program may use at most 128 MiB of HBM per device.

```python
import jax
import jax.numpy as jnp
from jax import lax

CLUSTER = 512
RMAX = 96
RMIN = 32
RHS = 256
NEAR_DEV = 8
FAR_DEV = 4
DIRS = 2048
NU = 32768
N_ROW = 8
N_COL = 8
DEVICES = 128


def cluster_pairs(key, per_device):
    total = DEVICES * per_device
    slots = jnp.arange(total, dtype=jnp.int32)
    device_pos = slots // per_device
    row_group = device_pos // N_COL % N_ROW
    col_group = device_pos % N_COL
    first_key, second_key = jax.random.split(key)
    rows = row_group * N_COL + jax.random.randint(first_key, (total,), 0, N_COL, dtype=jnp.int32)
    cols = col_group * N_ROW + jax.random.randint(second_key, (total,), 0, N_ROW, dtype=jnp.int32)
    last_slot = (DEVICES - 1) * per_device
    rows = rows.at[0].set(0).at[last_slot].set(N_ROW * N_COL - 1)
    cols = cols.at[0].set(0).at[last_slot].set(N_ROW * N_COL - 1)
    return jnp.stack([rows, cols], axis=1).astype(jnp.int32)


def draw_near_pairs(key, part):
    return cluster_pairs(jax.random.fold_in(key, 11), NEAR_DEV)


def draw_far_pairs(key, part):
    return cluster_pairs(jax.random.fold_in(key, 23), FAR_DEV)


def draw_far_ranks(key, part):
    total = DEVICES * FAR_DEV
    ranks = jax.random.randint(jax.random.fold_in(key, 37), (total,), RMIN, RMAX + 1, dtype=jnp.int32)
    ranks = ranks.at[0].set(RMAX).at[FAR_DEV].set(RMIN)
    return ranks.astype(jnp.int32)


def skewed_counts(key, most):
    first_key, second_key = jax.random.split(key)
    chosen = jax.random.randint(first_key, (DEVICES,), 0, 4, dtype=jnp.int32)
    counts = jnp.where(chosen == 0, most, max(1, most // 4)).astype(jnp.int32)
    forced = jax.random.randint(second_key, (), 0, DEVICES, dtype=jnp.int32)
    return counts.at[forced].set(most)


def draw_block_counts(key, part):
    near_counts = skewed_counts(jax.random.fold_in(key, 41), NEAR_DEV)
    far_counts = skewed_counts(jax.random.fold_in(key, 43), FAR_DEV)
    return jnp.stack([near_counts, far_counts], axis=1).astype(jnp.int32)


def shard_levels(key, dims, cuts, smallest, largest):
    gain = 1.0
    for dim, shards_of in cuts:
        steps = jax.random.uniform(jax.random.fold_in(jax.random.fold_in(key, 6), dim), (shards_of,), jnp.float32, smallest / len(cuts), largest / len(cuts))
        gain = gain * jnp.repeat(jnp.exp(steps), dims[dim] // shards_of).reshape((-1,) + (1,) * (len(dims) - 1 - dim))
    return gain


def scatter_about(key, extent, spread, reach, shards=(), held_as=jnp.bfloat16):
    array = jax.random.normal(key, extent, jnp.float32) * spread
    if len(shards) > 0:
        array = shard_levels(key, extent, shards, -0.22, 0.18) * array
    return jnp.clip(array, min=-reach, max=reach).astype(held_as)


def setup_inputs(seed: int = 0) -> dict:
    streams_of = jax.random.split(jax.random.key(seed), 10)
    return {
        "cotangent": scatter_about(streams_of[0], (DIRS, 2 * RHS), 0.5, 3.0, ((0, 2),)),
        "radiation": scatter_about(streams_of[1], (2, NU, DIRS), DIRS ** -0.5, 0.125, ((1, 64), (2, 2))),
        "near_z": scatter_about(streams_of[2], (2, DEVICES * NEAR_DEV, CLUSTER, CLUSTER), CLUSTER ** -0.5, 0.25, ((1, 128),), jnp.float32),
        "near_pairs": draw_near_pairs(jax.random.fold_in(streams_of[9], 71), 0),
        "far_ut": scatter_about(streams_of[4], (2, DEVICES * FAR_DEV, RMAX, CLUSTER), CLUSTER ** -0.5, 0.25, ((1, 128),), jnp.float32),
        "far_vt": scatter_about(streams_of[5], (2, DEVICES * FAR_DEV, RMAX, CLUSTER), RMAX ** -0.5, 0.625, ((1, 128),), jnp.float32),
        "far_pairs": draw_far_pairs(jax.random.fold_in(streams_of[9], 71), 0),
        "far_ranks": draw_far_ranks(jax.random.fold_in(streams_of[9], 71), 0),
        "block_counts": draw_block_counts(jax.random.fold_in(streams_of[9], 71), 0),
    }


def swap_parts(values):
    half_width = values.shape[1] // 2
    return jnp.concatenate([-values[:, half_width:], values[:, :half_width]], axis=1)


def transposed_dot(left, right):
    return lax.dot_general(left, right, (((0,), (0,)), ((), ())), precision=lax.Precision.HIGHEST, preferred_element_type=jnp.float32)


def plain_dot(left, right):
    return jnp.dot(left, right, precision=lax.Precision.HIGHEST, preferred_element_type=jnp.float32)


def add_rows(total, term, start):
    current = lax.dynamic_slice_in_dim(total, start, term.shape[0], 0)
    return lax.dynamic_update_slice_in_dim(total, current + term, start, 0)


def reference(cotangent, radiation, near_z, near_pairs, far_ut, far_vt, far_pairs, far_ranks, block_counts):
    rhs_full = jnp.dot(radiation[0], cotangent, preferred_element_type=jnp.float32) + jnp.dot(radiation[1], swap_parts(cotangent), preferred_element_type=jnp.float32)
    rhs_swap = swap_parts(rhs_full)
    rank_most = far_ut.shape[2]

    def near_step(slot_index, total):
        slot_index = jnp.asarray(slot_index).astype(jnp.int32)
        device_pos = slot_index // NEAR_DEV
        live = (slot_index % NEAR_DEV) < block_counts[device_pos, 0]

        def apply_block(total):
            row_start = (near_pairs[slot_index, 0] * CLUSTER).astype(jnp.int32)
            col_start = (near_pairs[slot_index, 1] * CLUSTER).astype(jnp.int32)
            source = lax.dynamic_slice_in_dim(rhs_full, row_start, CLUSTER, 0)
            source_swap = lax.dynamic_slice_in_dim(rhs_swap, row_start, CLUSTER, 0)
            blocks = near_z[:, slot_index]
            term = transposed_dot(blocks[0], source) + transposed_dot(blocks[1], source_swap)
            return add_rows(total, term, col_start)

        return lax.cond(live, apply_block, lambda kept: kept, total)

    def far_step(slot_index, total):
        slot_index = jnp.asarray(slot_index).astype(jnp.int32)
        device_pos = slot_index // FAR_DEV
        live = (slot_index % FAR_DEV) < block_counts[device_pos, 1]

        def apply_block(total):
            row_start = (far_pairs[slot_index, 0] * CLUSTER).astype(jnp.int32)
            col_start = (far_pairs[slot_index, 1] * CLUSTER).astype(jnp.int32)
            source = lax.dynamic_slice_in_dim(rhs_full, row_start, CLUSTER, 0)
            source_swap = lax.dynamic_slice_in_dim(rhs_swap, row_start, CLUSTER, 0)
            left_f = far_ut[:, slot_index]
            right_f = far_vt[:, slot_index]
            coeffs = plain_dot(left_f[0], source) + plain_dot(left_f[1], source_swap)
            keep_rows = (lax.iota(jnp.int32, rank_most) < far_ranks[slot_index])[:, None]
            coeffs = jnp.where(keep_rows, coeffs, jnp.zeros_like(coeffs))
            term = transposed_dot(right_f[0], coeffs) + transposed_dot(right_f[1], swap_parts(coeffs))
            return add_rows(total, term, col_start)

        return lax.cond(live, apply_block, lambda kept: kept, total)

    total = jnp.zeros(rhs_full.shape, jnp.float32)
    total = lax.fori_loop(0, near_pairs.shape[0], near_step, total)
    total = lax.fori_loop(0, far_pairs.shape[0], far_step, total)
    return total
```

```python
import functools

import jax
import jax.numpy as jnp
from jax import lax
from jax.experimental import pallas as pl
from jax.experimental.pallas import tpu as pltpu
from jax.sharding import Mesh
from jax.sharding import PartitionSpec as P

AXES = ("dir", "y", "zhi", "x", "core")
ROW = ("y", "zhi")
COL = ("x", "core")
SIZES = (2, 4, 2, 4, 2)
CHUNKS = 2
CLUSTER = 512
HALF = 128
WIDE = 2 * HALF
PAD = 128
NEAR = 8
FAR = 4
VMEM_LIMIT = 48 << 20

ANY = pl.BlockSpec(memory_space=pl.ANY)
SMEM = pl.BlockSpec(memory_space=pltpu.SMEM)

N_NEAR, N_FAR, NEAR_A, NEAR_B, FAR_A, FAR_B, RANK, ORDER = 0, 1, 2, 10, 18, 22, 26, 30


def split(values):
    high = values.astype(jnp.bfloat16)
    low = (values - high.astype(jnp.float32)).astype(jnp.bfloat16)
    return high, low


def dot(left, right):
    return jnp.dot(left, right, preferred_element_type=jnp.float32)


def rotations():
    tables = []
    for first in (True, False):
        for shift in (1, 2, 3):
            pairs = []
            for lo in range(2):
                for y in range(4):
                    for hi in range(2):
                        for x in range(4):
                            for core in range(2):
                                z = hi * 2 + lo
                                if (core == 0) == first:
                                    to_y, to_z = (y + shift) % 4, z
                                else:
                                    to_y, to_z = y, (z + shift) % 4
                                here = (((lo * 4 + y) * 2 + hi) * 4 + x) * 2 + core
                                there = (((to_z % 2 * 4 + to_y) * 2 + to_z // 2) * 4 + x) * 2 + core
                                pairs.append((here, there))
            tables.append(pairs)
    return tables[:3], tables[3:]


def rhs_kernel(cot_ref, rad_ref, *out_refs):
    width = cot_ref.shape[1] // 2
    for chunk, out_ref in enumerate(out_refs):
        re = cot_ref[:, chunk * HALF : (chunk + 1) * HALF]
        im = cot_ref[:, width + chunk * HALF : width + (chunk + 1) * HALF]
        out_ref[...] = dot(rad_ref[0], jnp.concatenate([re, im], 1)) + dot(
            rad_ref[1], jnp.concatenate([-im, re], 1)
        )


def partial_rhs(cotangent, radiation):
    _, rows, dirs = radiation.shape
    tile = 128
    return pl.pallas_call(
        rhs_kernel,
        name="rhs",
        grid=(rows // tile,),
        in_specs=[
            pl.BlockSpec(cotangent.shape, lambda i: (0, 0)),
            pl.BlockSpec((2, tile, dirs), lambda i: (0, i, 0)),
        ],
        out_specs=[pl.BlockSpec((tile, WIDE), lambda i: (i, 0))] * CHUNKS,
        out_shape=[jax.ShapeDtypeStruct((rows, WIDE), jnp.float32)] * CHUNKS,
        compiler_params=pltpu.CompilerParams(vmem_limit_bytes=VMEM_LIMIT),
        cost_estimate=pl.CostEstimate(flops=1 << 30, bytes_accessed=4 << 20, transcendentals=0),
    )(cotangent, radiation)


def prepare_kernel(table, z_ref, u_ref, v_ref, z_out, u_out, v_out, z_in, z_buf, u_in, u_buf, v_in, v_buf, sem_in, sem_out, sem_u, sem_v, sem_uo, sem_vo):
    near, far = table[N_NEAR], table[N_FAR]

    def fetch(s, b):
        return pltpu.make_async_copy(z_ref.at[:, s], z_in.at[b], sem_in.at[b])

    def keep(s, b):
        return pltpu.make_async_copy(z_buf.at[b], z_out.at[s], sem_out.at[b])

    fetch(0, 0).start()

    def near_step(s, _):
        b = lax.rem(s, 2)
        fetch(s, b).wait()

        @pl.when(s + 1 < near)
        def _():
            fetch(s + 1, 1 - b).start()

        @pl.when(s >= 2)
        def _():
            keep(s - 2, b).wait()

        for part in range(2):
            high, low = split(z_in[b, part].T)
            z_buf[b, :, part * CLUSTER : (part + 1) * CLUSTER] = high
            z_buf[b, :, (part + 2) * CLUSTER : (part + 3) * CLUSTER] = low
        keep(s, b).start()
        return 0

    lax.fori_loop(0, near, near_step, 0)

    @pl.when(near >= 2)
    def _():
        keep(near - 2, lax.rem(near, 2)).wait()

    keep(near - 1, lax.rem(near - 1, 2)).wait()

    rank_most = u_in.shape[1]
    u_buf[...] = jnp.zeros_like(u_buf)
    v_buf[...] = jnp.zeros_like(v_buf)

    def far_step(s, _):
        copies = (
            pltpu.make_async_copy(u_ref.at[:, s], u_in, sem_u),
            pltpu.make_async_copy(v_ref.at[:, s], v_in, sem_v),
        )
        for copy in copies:
            copy.start()
        for copy in copies:
            copy.wait()
        live = lax.broadcasted_iota(jnp.int32, u_in.shape[1:], 0) < table[RANK + s]
        for part in range(2):
            high, low = split(jnp.where(live, u_in[part], 0.0))
            u_buf[:rank_most, part * CLUSTER : (part + 1) * CLUSTER] = high
            u_buf[:rank_most, (part + 2) * CLUSTER : (part + 3) * CLUSTER] = low
            padded = jnp.concatenate([v_in[part], jnp.zeros((PAD - rank_most, CLUSTER), jnp.float32)], 0)
            high, low = split(padded.T)
            v_buf[:, part * PAD : (part + 1) * PAD] = high
            v_buf[:, (part + 2) * PAD : (part + 3) * PAD] = low
        copies = (
            pltpu.make_async_copy(u_buf, u_out.at[s], sem_uo),
            pltpu.make_async_copy(v_buf, v_out.at[s], sem_vo),
        )
        for copy in copies:
            copy.start()
        for copy in copies:
            copy.wait()
        return 0

    lax.fori_loop(0, far, far_step, 0)


def prepare(table, near_z, far_ut, far_vt):
    bf16 = jnp.bfloat16
    rank_most = far_ut.shape[2]
    return pl.pallas_call(
        prepare_kernel,
        name="prepare",
        in_specs=[SMEM, ANY, ANY, ANY],
        out_specs=[ANY, ANY, ANY],
        out_shape=[
            jax.ShapeDtypeStruct((NEAR, CLUSTER, 4 * CLUSTER), bf16),
            jax.ShapeDtypeStruct((FAR, PAD, 4 * CLUSTER), bf16),
            jax.ShapeDtypeStruct((FAR, CLUSTER, 4 * PAD), bf16),
        ],
        scratch_shapes=[
            pltpu.VMEM((2, 2, CLUSTER, CLUSTER), jnp.float32),
            pltpu.VMEM((2, CLUSTER, 4 * CLUSTER), bf16),
            pltpu.VMEM((2, rank_most, CLUSTER), jnp.float32),
            pltpu.VMEM((PAD, 4 * CLUSTER), bf16),
            pltpu.VMEM((2, rank_most, CLUSTER), jnp.float32),
            pltpu.VMEM((CLUSTER, 4 * PAD), bf16),
            pltpu.SemaphoreType.DMA((2,)),
            pltpu.SemaphoreType.DMA((2,)),
            pltpu.SemaphoreType.DMA,
            pltpu.SemaphoreType.DMA,
            pltpu.SemaphoreType.DMA,
            pltpu.SemaphoreType.DMA,
        ],
        compiler_params=pltpu.CompilerParams(vmem_limit_bytes=VMEM_LIMIT),
        cost_estimate=pl.CostEstimate(flops=1 << 30, bytes_accessed=36 << 20, transcendentals=0),
    )(table, near_z, far_ut, far_vt)


def parts_of(values):
    high, low = split(values)
    high = jnp.concatenate([high, jnp.concatenate([-high[:, HALF:], high[:, :HALF]], 1)], 0)
    low = jnp.concatenate([low, jnp.concatenate([-low[:, HALF:], low[:, :HALF]], 1)], 0)
    return high, low


def product(left, values):
    high, low = parts_of(values)
    return dot(left, jnp.concatenate([high, high], 0)) + dot(left[:, : left.shape[1] // 2], low)


def apply_kernel(table, x_ref, z_ref, u_ref, v_ref, *rest):
    outs, (total, z_buf, x_buf, u_buf, v_buf, fx_buf, sem_z, sem_x, sem_u, sem_v, sem_fx, sem_out) = rest[:4], rest[4:]
    near, far = table[N_NEAR], table[N_FAR]

    def fetch(s, b):
        return (
            pltpu.make_async_copy(z_ref.at[s], z_buf.at[b], sem_z.at[b]),
            pltpu.make_async_copy(x_ref.at[table[NEAR_A + s]], x_buf.at[b], sem_x.at[b]),
        )

    def fetch_far(s):
        return (
            pltpu.make_async_copy(u_ref.at[s], u_buf.at[s], sem_u.at[s]),
            pltpu.make_async_copy(v_ref.at[s], v_buf.at[s], sem_v.at[s]),
            pltpu.make_async_copy(x_ref.at[table[FAR_A + s]], fx_buf.at[s], sem_fx.at[s]),
        )

    for copy in fetch(0, 0):
        copy.start()

    def far_start(s, _):
        for copy in fetch_far(s):
            copy.start()
        return 0

    lax.fori_loop(0, far, far_start, 0)
    total[...] = jnp.zeros_like(total)

    def near_step(s, _):
        b = lax.rem(s, 2)

        @pl.when(s + 1 < near)
        def _():
            for copy in fetch(s + 1, 1 - b):
                copy.start()

        for copy in fetch(s, b):
            copy.wait()
        total[table[NEAR_B + s]] += product(z_buf[b], x_buf[b])
        return 0

    lax.fori_loop(0, near, near_step, 0)

    def far_step(s, _):
        for copy in fetch_far(s):
            copy.wait()
        coeffs = product(u_buf[s], fx_buf[s])
        total[table[FAR_B + s]] += product(v_buf[s], coeffs)
        return 0

    lax.fori_loop(0, far, far_step, 0)

    copies = []
    for first in range(4):
        for second in range(4):
            place = table[ORDER + first * 4 + second]
            source = total.at[place // 2, pl.ds(pl.multiple_of(lax.rem(place, 2) * (CLUSTER // 2), CLUSTER // 2), CLUSTER // 2)]
            copies.append(pltpu.make_async_copy(source, outs[first].at[second], sem_out.at[first * 4 + second]))
    for copy in copies:
        copy.start()
    for copy in copies:
        copy.wait()


def apply_blocks(table, x, z, u, v, index):
    bf16 = jnp.bfloat16
    return pl.pallas_call(
        apply_kernel,
        name=f"apply_{index}",
        in_specs=[SMEM, ANY, ANY, ANY, ANY],
        out_specs=[ANY] * 4,
        out_shape=[jax.ShapeDtypeStruct((4, CLUSTER // 2, WIDE), jnp.float32)] * 4,
        scratch_shapes=[
            pltpu.VMEM((8, CLUSTER, WIDE), jnp.float32),
            pltpu.VMEM((2, CLUSTER, 4 * CLUSTER), bf16),
            pltpu.VMEM((2, CLUSTER, WIDE), jnp.float32),
            pltpu.VMEM((FAR, PAD, 4 * CLUSTER), bf16),
            pltpu.VMEM((FAR, CLUSTER, 4 * PAD), bf16),
            pltpu.VMEM((FAR, CLUSTER, WIDE), jnp.float32),
            pltpu.SemaphoreType.DMA((2,)),
            pltpu.SemaphoreType.DMA((2,)),
            pltpu.SemaphoreType.DMA((FAR,)),
            pltpu.SemaphoreType.DMA((FAR,)),
            pltpu.SemaphoreType.DMA((FAR,)),
            pltpu.SemaphoreType.DMA((16,)),
        ],
        compiler_params=pltpu.CompilerParams(vmem_limit_bytes=VMEM_LIMIT),
        cost_estimate=pl.CostEstimate(flops=12 << 30, bytes_accessed=32 << 20, transcendentals=0),
    )(table, x, z, u, v)


def scalars(near_pairs, far_pairs, far_ranks, block_counts):
    row_base = lax.axis_index(ROW) * 8
    col_base = lax.axis_index(COL) * 8
    core = lax.axis_index("core")
    index = lax.iota(jnp.int32, 16)
    first, second = index // 4, index % 4
    y = (lax.axis_index("y") + jnp.where(core == 0, first, second)) % 4
    z = (lax.axis_index("zhi") * 2 + lax.axis_index("dir") + jnp.where(core == 0, second, first)) % 4
    order = (z % 2 * 4 + y) * 2 + z // 2
    pieces = [
        block_counts[0],
        near_pairs[:, 0] - row_base,
        near_pairs[:, 1] - col_base,
        far_pairs[:, 0] - row_base,
        far_pairs[:, 1] - col_base,
        far_ranks,
        order,
    ]
    return jnp.concatenate(pieces).astype(jnp.int32)


def shards(cotangent, radiation, near_z, near_pairs, far_ut, far_vt, far_pairs, far_ranks, block_counts):
    first_turn, second_turn = rotations()
    table = scalars(near_pairs, far_pairs, far_ranks, block_counts)
    partial = partial_rhs(cotangent, radiation)
    swap_dir = [(0, 1), (1, 0)]

    gathered = []
    for chunk in range(CHUNKS):
        own = partial[chunk]
        if chunk > 0:
            own = lax.optimization_barrier((own, rhs))[0]
        rhs = own + lax.ppermute(own, "dir", swap_dir)
        gathered.append(lax.all_gather(rhs, COL, axis=0, tiled=False))
    blocks = prepare(table, near_z, far_ut, far_vt)

    results = []
    for chunk in range(CHUNKS):
        mine, *others = apply_blocks(table, gathered[chunk], *blocks, chunk)
        came = [lax.ppermute(part, AXES, turn) for part, turn in zip(others, first_turn)]
        sums = [mine[k] + came[0][k] + came[1][k] + came[2][k] for k in range(4)]
        came = [lax.ppermute(part, AXES, turn) for part, turn in zip(sums[1:], second_turn)]
        results.append(sums[0] + came[0] + came[1] + came[2])
    parts = [r[:, :HALF] for r in results] + [r[:, HALF:] for r in results]
    return jnp.concatenate(parts, axis=1)


def solution(mesh):
    finer = Mesh(mesh.devices.reshape(SIZES), AXES)
    blocks = P(None, AXES, None, None)
    in_specs = (
        P("dir", None),
        P(None, ("y", "zhi", "x", "core"), "dir"),
        blocks,
        P(AXES, None),
        blocks,
        blocks,
        P(AXES, None),
        P(AXES),
        P(AXES, None),
    )
    out_specs = P(("x", "core", "dir", "y", "zhi"), None)
    return jax.shard_map(shards, mesh=finer, in_specs=in_specs, out_specs=out_specs, check_vma=False)
```

```python
import functools

import jax
import jax.numpy as jnp
from jax import lax
from jax.experimental import pallas as pl
from jax.experimental.pallas import tpu as pltpu
from jax.sharding import Mesh
from jax.sharding import PartitionSpec as P

AXES = ("dir", "y", "zhi", "x", "core")
ROW = ("y", "zhi")
COL = ("x", "core")
SIZES = (2, 4, 2, 4, 2)
CHUNKS = 2
CLUSTER = 512
HALF = 128
WIDE = 2 * HALF
PAD = 128
NEAR = 8
FAR = 4
VMEM_LIMIT = 60 << 20
SCOPED = 14 << 20

ANY = pl.BlockSpec(memory_space=pl.ANY)
SMEM = pl.BlockSpec(memory_space=pltpu.SMEM)
VMEM = pl.BlockSpec(memory_space=pltpu.VMEM)
TOKEN = jax.ShapeDtypeStruct((8, 128), jnp.float32)

N_NEAR, N_FAR, NEAR_A, NEAR_B, FAR_A, FAR_B, RANK, ORDER, CORE, X = 0, 1, 2, 10, 18, 22, 26, 30, 46, 47


def split(values):
    high = values.astype(jnp.bfloat16)
    low = (values - high.astype(jnp.float32)).astype(jnp.bfloat16)
    return high, low


def dot(left, right):
    return jnp.dot(left, right, preferred_element_type=jnp.float32)


def rings(first):
    def place(y, z, core):
        return ((z % 2 * 4 + y) * 2 + z // 2) * 2 + core

    round_y, round_z = (0, 1) if first else (1, 0)
    along_y = [[place(y, z, round_y) for y in range(4)] for z in range(4)]
    along_z = [[place(y, z, round_z) for z in range(4)] for y in range(4)]
    return along_y + along_z


def rhs_kernel(cot_ref, rad_ref, *out_refs):
    width = cot_ref.shape[1] // 2
    for chunk, out_ref in enumerate(out_refs):
        re = cot_ref[:, chunk * HALF : (chunk + 1) * HALF]
        im = cot_ref[:, width + chunk * HALF : width + (chunk + 1) * HALF]
        out_ref[...] = dot(rad_ref[0], jnp.concatenate([re, im], 1)) + dot(
            rad_ref[1], jnp.concatenate([-im, re], 1)
        )


def partial_rhs(cotangent, radiation):
    _, rows, dirs = radiation.shape
    tile = 128
    return pl.pallas_call(
        rhs_kernel,
        name="rhs",
        grid=(rows // tile,),
        in_specs=[
            pl.BlockSpec(cotangent.shape, lambda i: (0, 0)),
            pl.BlockSpec((2, tile, dirs), lambda i: (0, i, 0)),
        ],
        out_specs=[pl.BlockSpec((tile, WIDE), lambda i: (i, 0))] * CHUNKS,
        out_shape=[jax.ShapeDtypeStruct((rows, WIDE), jnp.float32)] * CHUNKS,
        compiler_params=pltpu.CompilerParams(vmem_limit_bytes=VMEM_LIMIT),
        cost_estimate=pl.CostEstimate(flops=1 << 30, bytes_accessed=4 << 20, transcendentals=0),
    )(cotangent, radiation)


def prepare_near_kernel(first, table, z_ref, out_ref, token, z_in, sem_in):
    slots, buffers = out_ref.shape[0], z_in.shape[0]
    token[...] = jnp.zeros_like(token)
    live = jnp.clip(table[N_NEAR] - first, 0, slots)

    def fetch(s):
        b = lax.rem(s, buffers)
        return pltpu.make_async_copy(z_ref.at[:, first + s], z_in.at[b], sem_in.at[b])

    for ahead in range(buffers - 1):

        @pl.when(ahead < live)
        def _():
            fetch(ahead).start()

    def near_step(s, _):
        @pl.when(s + buffers - 1 < live)
        def _():
            fetch(s + buffers - 1).start()

        fetch(s).wait()
        for part in range(2):
            high, low = split(z_in[lax.rem(s, buffers), part].T)
            out_ref[s, :, part * CLUSTER : (part + 1) * CLUSTER] = high
            out_ref[s, :, (part + 2) * CLUSTER : (part + 3) * CLUSTER] = low
        return 0

    lax.fori_loop(0, live, near_step, 0)


def prepare_near(table, near_z, first, slots):
    buffers = 3
    return pl.pallas_call(
        functools.partial(prepare_near_kernel, first),
        name=f"prepare_near_{first}",
        in_specs=[SMEM, ANY],
        out_specs=[VMEM, VMEM],
        out_shape=[pltpu.VMEM((slots, CLUSTER, 4 * CLUSTER), jnp.bfloat16), TOKEN],
        scratch_shapes=[
            pltpu.VMEM((buffers, 2, CLUSTER, CLUSTER), jnp.float32),
            pltpu.SemaphoreType.DMA((buffers,)),
        ],
        compiler_params=pltpu.CompilerParams(vmem_limit_bytes=SCOPED),
        cost_estimate=pl.CostEstimate(flops=1 << 28, bytes_accessed=slots << 21, transcendentals=0),
    )(table, near_z)


def prepare_far_kernel(table, u_ref, v_ref, u_out, v_out, token, u_in, v_in, sem_u, sem_v):
    token[...] = jnp.zeros_like(token)
    far, rank_most = table[N_FAR], u_in.shape[2]

    def fetch(s):
        return (
            pltpu.make_async_copy(u_ref.at[:, s], u_in.at[s], sem_u.at[s]),
            pltpu.make_async_copy(v_ref.at[:, s], v_in.at[s], sem_v.at[s]),
        )

    def start(s, _):
        for copy in fetch(s):
            copy.start()
        return 0

    lax.fori_loop(0, far, start, 0)

    def far_step(s, _):
        for copy in fetch(s):
            copy.wait()
        live = lax.broadcasted_iota(jnp.int32, (PAD, CLUSTER), 0) < table[RANK + s]
        fill = jnp.zeros((PAD - rank_most, CLUSTER), jnp.float32)
        for part in range(2):
            padded = jnp.concatenate([u_in[s, part], fill], 0)
            high, low = split(jnp.where(live, padded, 0.0))
            u_out[s, :, part * CLUSTER : (part + 1) * CLUSTER] = high
            u_out[s, :, (part + 2) * CLUSTER : (part + 3) * CLUSTER] = low
            padded = jnp.concatenate([v_in[s, part], fill], 0)
            high, low = split(padded.T)
            v_out[s, :, part * PAD : (part + 1) * PAD] = high
            v_out[s, :, (part + 2) * PAD : (part + 3) * PAD] = low
        return 0

    lax.fori_loop(0, far, far_step, 0)


def prepare_far(table, far_ut, far_vt):
    rank_most = far_ut.shape[2]
    return pl.pallas_call(
        prepare_far_kernel,
        name="prepare_far",
        in_specs=[SMEM, ANY, ANY],
        out_specs=[VMEM, VMEM, VMEM],
        out_shape=[
            pltpu.VMEM((FAR, PAD, 4 * CLUSTER), jnp.bfloat16),
            pltpu.VMEM((FAR, CLUSTER, 4 * PAD), jnp.bfloat16),
            TOKEN,
        ],
        scratch_shapes=[
            pltpu.VMEM((FAR, 2, rank_most, CLUSTER), jnp.float32),
            pltpu.VMEM((FAR, 2, rank_most, CLUSTER), jnp.float32),
            pltpu.SemaphoreType.DMA((FAR,)),
            pltpu.SemaphoreType.DMA((FAR,)),
        ],
        compiler_params=pltpu.CompilerParams(vmem_limit_bytes=SCOPED),
        cost_estimate=pl.CostEstimate(flops=1 << 28, bytes_accessed=4 << 20, transcendentals=0),
    )(table, far_ut, far_vt)


def parts_of(values):
    high, low = split(values)
    high = jnp.concatenate([high, jnp.concatenate([-high[:, HALF:], high[:, :HALF]], 1)], 0)
    low = jnp.concatenate([low, jnp.concatenate([-low[:, HALF:], low[:, :HALF]], 1)], 0)
    return high, low


def product(left, values):
    high, low = parts_of(values)
    return dot(left, jnp.concatenate([high, high], 0)) + dot(left[:, : left.shape[1] // 2], low)


def apply_kernel(table, *refs):
    held, (za_ref, zb_ref, u_ref, v_ref, out_ref, x_buf, fx_buf, sem_x, sem_fx) = refs[:8], refs[8:]
    near, far = table[N_NEAR], table[N_FAR]
    slots = za_ref.shape[0]

    def fetch(cluster, buf, sem):
        steps = lax.rem(table[X] + 4 - cluster // 2, 4)
        other = jnp.where(lax.rem(cluster, 2) == table[CORE], 0, 4)
        for place, ref in enumerate(held):

            @pl.when(steps + other == place)
            def _():
                pltpu.make_async_copy(ref, buf, sem).start()

    def fetched(buf, sem):
        pltpu.make_async_copy(held[0], buf, sem).wait()

    def add(cluster, term):
        for half in range(2):
            rows = CLUSTER // 2
            out_ref[table[ORDER + cluster * 2 + half]] += term[half * rows : (half + 1) * rows]

    fetch(table[NEAR_A], x_buf.at[0], sem_x.at[0])

    def far_start(s, _):
        fetch(table[FAR_A + s], fx_buf.at[s], sem_fx.at[s])
        return 0

    lax.fori_loop(0, far, far_start, 0)
    out_ref[...] = jnp.zeros_like(out_ref)

    def near_steps(z_ref, first, last):
        def near_step(s, _):
            b = lax.rem(s, 2)

            @pl.when(s + 1 < near)
            def _():
                fetch(table[NEAR_A + s + 1], x_buf.at[1 - b], sem_x.at[1 - b])

            fetched(x_buf.at[b], sem_x.at[b])
            add(table[NEAR_B + s], product(z_ref[s - first], x_buf[b]))
            return 0

        lax.fori_loop(first, last, near_step, 0)

    near_steps(za_ref, 0, jnp.minimum(near, slots))
    near_steps(zb_ref, slots, near)

    def far_step(s, _):
        fetched(fx_buf.at[s], sem_fx.at[s])
        add(table[FAR_B + s], product(v_ref[s], product(u_ref[s], fx_buf[s])))
        return 0

    lax.fori_loop(0, far, far_step, 0)


def apply_blocks(table, held, blocks, index):
    return pl.pallas_call(
        apply_kernel,
        name=f"apply_{index}",
        in_specs=[SMEM] + [ANY] * 8 + [VMEM] * 4,
        out_specs=VMEM,
        out_shape=pltpu.VMEM((16, CLUSTER // 2, WIDE), jnp.float32),
        scratch_shapes=[
            pltpu.VMEM((2, CLUSTER, WIDE), jnp.float32),
            pltpu.VMEM((FAR, CLUSTER, WIDE), jnp.float32),
            pltpu.SemaphoreType.DMA((2,)),
            pltpu.SemaphoreType.DMA((FAR,)),
        ],
        compiler_params=pltpu.CompilerParams(vmem_limit_bytes=SCOPED),
        cost_estimate=pl.CostEstimate(flops=8 << 30, bytes_accessed=8 << 20, transcendentals=0),
    )(table, *held, *blocks)


def scalars(near_pairs, far_pairs, far_ranks, block_counts):
    row_base = lax.axis_index(ROW) * 8
    col_base = lax.axis_index(COL) * 8
    core = lax.axis_index("core")
    index = lax.iota(jnp.int32, 16)
    y = index // 2 % 4
    z = index % 2 * 2 + index // 8
    order = jnp.where(core == 0, y * 4 + z, z * 4 + y)
    pieces = [
        block_counts[0],
        near_pairs[:, 0] - row_base,
        near_pairs[:, 1] - col_base,
        far_pairs[:, 0] - row_base,
        far_pairs[:, 1] - col_base,
        far_ranks,
        order,
        core[None],
        lax.axis_index("x")[None],
    ]
    return jnp.concatenate(pieces).astype(jnp.int32)


def exchange(values, axes, groups=None):
    return lax.all_to_all(values, axes, split_axis=0, concat_axis=0, tiled=True, axis_index_groups=groups)


def shards(cotangent, radiation, near_z, near_pairs, far_ut, far_vt, far_pairs, far_ranks, block_counts):
    table = scalars(near_pairs, far_pairs, far_ranks, block_counts)
    own_0, own_1 = partial_rhs(cotangent, radiation)
    swap = [(0, 1), (1, 0)]
    plane = ("dir", "y", "zhi", "core")

    def others(own):
        return [lax.ppermute(own, "x", [(i, (i + k) % 4) for i in range(4)]) for k in (1, 2, 3)]

    def both_cores(mine):
        return mine + [lax.ppermute(part, "core", swap) for part in mine]

    blocks_a, done_a = prepare_near(table, near_z, 0, NEAR // 2)
    own_0 = own_0 + (lax.ppermute(own_0, "dir", swap) + done_a[0, 0])
    own_0, own_1 = lax.optimization_barrier((own_0, own_1))
    around_0 = others(own_0)
    blocks_b, done_b = prepare_near(table, near_z, NEAR // 2, NEAR // 2)
    blocks_u, blocks_v, done_far = prepare_far(table, far_ut, far_vt)
    own_1 = own_1 + (lax.ppermute(own_1, "dir", swap) + (done_b[0, 0] + done_far[0, 0]))
    own_1, *around_0 = lax.optimization_barrier((own_1, *around_0))
    held_0 = both_cores([own_0, *around_0])
    around_1 = others(own_1)
    blocks = (blocks_a, blocks_b, blocks_u, blocks_v)

    sums = []
    for chunk, held in enumerate((held_0, None)):
        if held is None:
            held = both_cores([own_1, *around_1])
        terms = apply_blocks(table, held, blocks, chunk).reshape(4, 4, CLUSTER // 2, WIDE)
        if chunk == 0:
            terms, *around_1 = lax.optimization_barrier((terms, *around_1))
        sums.append(exchange(terms, plane, rings(True)).sum(axis=0))
    result = exchange(jnp.stack(sums, axis=1), plane, rings(False)).sum(axis=0)
    parts = [r[:, :HALF] for r in result] + [r[:, HALF:] for r in result]
    return jnp.concatenate(parts, axis=1)


def solution(mesh):
    finer = Mesh(mesh.devices.reshape(SIZES), AXES)
    blocks = P(None, AXES, None, None)
    in_specs = (
        P("dir", None),
        P(None, ("y", "zhi", "x", "core"), "dir"),
        blocks,
        P(AXES, None),
        blocks,
        blocks,
        P(AXES, None),
        P(AXES),
        P(AXES, None),
    )
    out_specs = P(("x", "core", "dir", "y", "zhi"), None)
    return jax.shard_map(shards, mesh=finer, in_specs=in_specs, out_specs=out_specs, check_vma=False)
```

```python
import functools

import jax
import jax.numpy as jnp
from jax import lax
from jax.experimental import pallas as pl
from jax.experimental.pallas import tpu as pltpu
from jax.sharding import Mesh
from jax.sharding import PartitionSpec as P

AXES = ("dir", "y", "zhi", "x", "core")
ROW = ("y", "zhi")
COL = ("x", "core")
SIZES = (2, 4, 2, 4, 2)
CHUNKS = 2
CLUSTER = 512
HALF = 128
WIDE = 2 * HALF
PAD = 128
NEAR = 8
FAR = 4
VMEM_LIMIT = 60 << 20
SCOPED = 14 << 20

ANY = pl.BlockSpec(memory_space=pl.ANY)
SMEM = pl.BlockSpec(memory_space=pltpu.SMEM)
VMEM = pl.BlockSpec(memory_space=pltpu.VMEM)
HBM = pl.BlockSpec(memory_space=pltpu.HBM)
TOKEN = jax.ShapeDtypeStruct((8, 128), jnp.float32)

N_NEAR, N_FAR, NEAR_A, NEAR_B, FAR_A, FAR_B, RANK, ORDER, CORE, X = 0, 1, 2, 10, 18, 22, 26, 30, 46, 47


def split(values):
    high = values.astype(jnp.bfloat16)
    low = (values - high.astype(jnp.float32)).astype(jnp.bfloat16)
    return high, low


def dot(left, right):
    return jnp.dot(left, right, preferred_element_type=jnp.float32)


def rotations():
    tables = []
    for first in (True, False):
        for shift in (1, 2, 3):
            pairs = []
            for lo in range(2):
                for y in range(4):
                    for hi in range(2):
                        for x in range(4):
                            for core in range(2):
                                z = hi * 2 + lo
                                if (core == 0) == first:
                                    to_y, to_z = (y + shift) % 4, z
                                else:
                                    to_y, to_z = y, (z + shift) % 4
                                here = (((lo * 4 + y) * 2 + hi) * 4 + x) * 2 + core
                                there = (((to_z % 2 * 4 + to_y) * 2 + to_z // 2) * 4 + x) * 2 + core
                                pairs.append((here, there))
            tables.append(pairs)
    return tables[:3], tables[3:]


def rhs_kernel(cot_ref, rad_ref, *out_refs):
    width = cot_ref.shape[1] // 2
    first = pl.program_id(0) == 0
    for chunk, out_ref in enumerate(out_refs):
        re = cot_ref[:, chunk * HALF : (chunk + 1) * HALF]
        im = cot_ref[:, width + chunk * HALF : width + (chunk + 1) * HALF]
        term = dot(rad_ref[0], jnp.concatenate([re, im], 1)) + dot(
            rad_ref[1], jnp.concatenate([-im, re], 1)
        )

        @pl.when(first)
        def _():
            out_ref[...] = term

        @pl.when(jnp.logical_not(first))
        def _():
            out_ref[...] += term


def partial_rhs(cotangent, radiation):
    _, rows, dirs = radiation.shape
    tile = 256
    return pl.pallas_call(
        rhs_kernel,
        name="rhs",
        grid=(dirs // tile,),
        in_specs=[
            pl.BlockSpec((tile, cotangent.shape[1]), lambda i: (i, 0)),
            pl.BlockSpec((2, rows, tile), lambda i: (0, 0, i)),
        ],
        out_specs=[pl.BlockSpec((rows, WIDE), lambda i: (0, 0))] * CHUNKS,
        out_shape=[jax.ShapeDtypeStruct((rows, WIDE), jnp.float32)] * CHUNKS,
        compiler_params=pltpu.CompilerParams(vmem_limit_bytes=VMEM_LIMIT),
        cost_estimate=pl.CostEstimate(flops=1 << 30, bytes_accessed=4 << 20, transcendentals=0),
    )(cotangent, radiation)


def prepare_near_kernel(first, table, z_ref, out_ref, token, z_in, sem_in):
    slots, buffers = out_ref.shape[0], z_in.shape[0]
    token[...] = jnp.zeros_like(token)
    live = jnp.clip(table[N_NEAR] - first, 0, slots)

    def fetch(s):
        b = lax.rem(s, buffers)
        return pltpu.make_async_copy(z_ref.at[:, first + s], z_in.at[b], sem_in.at[b])

    for ahead in range(buffers - 1):

        @pl.when(ahead < live)
        def _():
            fetch(ahead).start()

    def near_step(s, _):
        @pl.when(s + buffers - 1 < live)
        def _():
            fetch(s + buffers - 1).start()

        fetch(s).wait()
        for part in range(2):
            high, low = split(z_in[lax.rem(s, buffers), part].T)
            out_ref[s, :, part * CLUSTER : (part + 1) * CLUSTER] = high
            out_ref[s, :, (part + 2) * CLUSTER : (part + 3) * CLUSTER] = low
        return 0

    lax.fori_loop(0, live, near_step, 0)


def prepare_near(table, near_z, first, slots):
    buffers = 3
    return pl.pallas_call(
        functools.partial(prepare_near_kernel, first),
        name=f"prepare_near_{first}",
        in_specs=[SMEM, HBM],
        out_specs=[VMEM, VMEM],
        out_shape=[pltpu.VMEM((slots, CLUSTER, 4 * CLUSTER), jnp.bfloat16), TOKEN],
        scratch_shapes=[
            pltpu.VMEM((buffers, 2, CLUSTER, CLUSTER), jnp.float32),
            pltpu.SemaphoreType.DMA((buffers,)),
        ],
        compiler_params=pltpu.CompilerParams(vmem_limit_bytes=SCOPED),
        cost_estimate=pl.CostEstimate(flops=1 << 28, bytes_accessed=slots << 21, transcendentals=0),
    )(table, pltpu.with_memory_space_constraint(near_z, pltpu.HBM))


def prepare_far_kernel(table, u_ref, v_ref, u_out, v_out, token, u_in, v_in, sem_u, sem_v):
    token[...] = jnp.zeros_like(token)
    far, rank_most = table[N_FAR], u_in.shape[2]

    def fetch(s):
        return (
            pltpu.make_async_copy(u_ref.at[:, s], u_in.at[s], sem_u.at[s]),
            pltpu.make_async_copy(v_ref.at[:, s], v_in.at[s], sem_v.at[s]),
        )

    def start(s, _):
        for copy in fetch(s):
            copy.start()
        return 0

    lax.fori_loop(0, far, start, 0)

    def far_step(s, _):
        for copy in fetch(s):
            copy.wait()
        live = lax.broadcasted_iota(jnp.int32, (PAD, CLUSTER), 0) < table[RANK + s]
        fill = jnp.zeros((PAD - rank_most, CLUSTER), jnp.float32)
        for part in range(2):
            padded = jnp.concatenate([u_in[s, part], fill], 0)
            high, low = split(jnp.where(live, padded, 0.0))
            u_out[s, :, part * CLUSTER : (part + 1) * CLUSTER] = high
            u_out[s, :, (part + 2) * CLUSTER : (part + 3) * CLUSTER] = low
            padded = jnp.concatenate([v_in[s, part], fill], 0)
            high, low = split(padded.T)
            v_out[s, :, part * PAD : (part + 1) * PAD] = high
            v_out[s, :, (part + 2) * PAD : (part + 3) * PAD] = low
        return 0

    lax.fori_loop(0, far, far_step, 0)


def prepare_far(table, far_ut, far_vt):
    rank_most = far_ut.shape[2]
    return pl.pallas_call(
        prepare_far_kernel,
        name="prepare_far",
        in_specs=[SMEM, HBM, HBM],
        out_specs=[VMEM, VMEM, VMEM],
        out_shape=[
            pltpu.VMEM((FAR, PAD, 4 * CLUSTER), jnp.bfloat16),
            pltpu.VMEM((FAR, CLUSTER, 4 * PAD), jnp.bfloat16),
            TOKEN,
        ],
        scratch_shapes=[
            pltpu.VMEM((FAR, 2, rank_most, CLUSTER), jnp.float32),
            pltpu.VMEM((FAR, 2, rank_most, CLUSTER), jnp.float32),
            pltpu.SemaphoreType.DMA((FAR,)),
            pltpu.SemaphoreType.DMA((FAR,)),
        ],
        compiler_params=pltpu.CompilerParams(vmem_limit_bytes=SCOPED),
        cost_estimate=pl.CostEstimate(flops=1 << 28, bytes_accessed=4 << 20, transcendentals=0),
    )(table, *(pltpu.with_memory_space_constraint(f, pltpu.HBM) for f in (far_ut, far_vt)))


def parts_of(values):
    high, low = split(values)
    high = jnp.concatenate([high, jnp.concatenate([-high[:, HALF:], high[:, :HALF]], 1)], 0)
    low = jnp.concatenate([low, jnp.concatenate([-low[:, HALF:], low[:, :HALF]], 1)], 0)
    return high, low


def product(left, values):
    high, low = parts_of(values)
    return dot(left, jnp.concatenate([high, high], 0)) + dot(left[:, : left.shape[1] // 2], low)


def apply_kernel(table, *refs):
    held, (za_ref, zb_ref, u_ref, v_ref), outs, (token, x_buf, fx_buf, sem_x, sem_fx) = refs[:8], refs[8:12], refs[12:16], refs[16:]
    near, far = table[N_NEAR], table[N_FAR]
    slots = za_ref.shape[0]

    def fetch(cluster, buf, sem):
        steps = lax.rem(table[X] + 4 - cluster // 2, 4)
        other = jnp.where(lax.rem(cluster, 2) == table[CORE], 0, 4)
        for place, ref in enumerate(held):

            @pl.when(steps + other == place)
            def _():
                pltpu.make_async_copy(ref, buf, sem).start()

    def fetched(buf, sem):
        pltpu.make_async_copy(held[0], buf, sem).wait()

    def add(cluster, term):
        for half in range(2):
            rows = CLUSTER // 2
            place = table[ORDER + cluster * 2 + half]
            for steps, out_ref in enumerate(outs):

                @pl.when(place // 4 == steps)
                def _():
                    out_ref[lax.rem(place, 4)] += term[half * rows : (half + 1) * rows]

    fetch(table[NEAR_A], x_buf.at[0], sem_x.at[0])

    def far_start(s, _):
        fetch(table[FAR_A + s], fx_buf.at[s], sem_fx.at[s])
        return 0

    lax.fori_loop(0, far, far_start, 0)
    for out_ref in (*outs, token):
        out_ref[...] = jnp.zeros_like(out_ref)

    def near_steps(z_ref, first, last):
        def near_step(s, _):
            b = lax.rem(s, 2)

            @pl.when(s + 1 < near)
            def _():
                fetch(table[NEAR_A + s + 1], x_buf.at[1 - b], sem_x.at[1 - b])

            fetched(x_buf.at[b], sem_x.at[b])
            add(table[NEAR_B + s], product(z_ref[s - first], x_buf[b]))
            return 0

        lax.fori_loop(first, last, near_step, 0)

    near_steps(za_ref, 0, jnp.minimum(near, slots))
    near_steps(zb_ref, slots, near)

    def far_step(s, _):
        fetched(fx_buf.at[s], sem_fx.at[s])
        add(table[FAR_B + s], product(v_ref[s], product(u_ref[s], fx_buf[s])))
        return 0

    lax.fori_loop(0, far, far_step, 0)


def apply_blocks(table, held, blocks, index):
    return pl.pallas_call(
        apply_kernel,
        name=f"apply_{index}",
        in_specs=[SMEM] + [ANY] * 8 + [VMEM] * 4,
        out_specs=[VMEM] * 5,
        out_shape=[jax.ShapeDtypeStruct((4, CLUSTER // 2, WIDE), jnp.float32)] * 4 + [TOKEN],
        scratch_shapes=[
            pltpu.VMEM((2, CLUSTER, WIDE), jnp.float32),
            pltpu.VMEM((FAR, CLUSTER, WIDE), jnp.float32),
            pltpu.SemaphoreType.DMA((2,)),
            pltpu.SemaphoreType.DMA((FAR,)),
        ],
        compiler_params=pltpu.CompilerParams(vmem_limit_bytes=SCOPED),
        cost_estimate=pl.CostEstimate(flops=40 << 30, bytes_accessed=8 << 20, transcendentals=0),
    )(table, *held, *blocks)


def scalars(near_pairs, far_pairs, far_ranks, block_counts):
    row_base = lax.axis_index(ROW) * 8
    col_base = lax.axis_index(COL) * 8
    core = lax.axis_index("core")
    index = lax.iota(jnp.int32, 16)
    steps_y = (index // 2 - lax.axis_index("y")) % 4
    steps_z = (index % 2 * 2 + index // 8 - lax.axis_index("zhi") * 2 - lax.axis_index("dir")) % 4
    order = jnp.where(core == 0, steps_y * 4 + steps_z, steps_z * 4 + steps_y)
    pieces = [
        block_counts[0],
        near_pairs[:, 0] - row_base,
        near_pairs[:, 1] - col_base,
        far_pairs[:, 0] - row_base,
        far_pairs[:, 1] - col_base,
        far_ranks,
        order,
        core[None],
        lax.axis_index("x")[None],
    ]
    return jnp.concatenate(pieces).astype(jnp.int32)


def shards(cotangent, radiation, near_z, near_pairs, far_ut, far_vt, far_pairs, far_ranks, block_counts):
    table = scalars(near_pairs, far_pairs, far_ranks, block_counts)
    own_0, own_1 = partial_rhs(cotangent, radiation)
    swap = [(0, 1), (1, 0)]
    first_turn, second_turn = rotations()

    def others(own):
        return [lax.ppermute(own, "x", [(i, (i + k) % 4) for i in range(4)]) for k in (1, 2, 3)]

    def both_cores(mine):
        return mine + [lax.ppermute(part, "core", swap) for part in mine]

    blocks_a, done_a = prepare_near(table, near_z, 0, NEAR // 2)
    own_0 = own_0 + (lax.ppermute(own_0, "dir", swap) + done_a[0, 0])
    own_0, own_1 = lax.optimization_barrier((own_0, own_1))
    around_0 = others(own_0)
    blocks_b, done_b = prepare_near(table, near_z, NEAR // 2, NEAR // 2)
    blocks_u, blocks_v, done_far = prepare_far(table, far_ut, far_vt)
    own_1 = own_1 + (lax.ppermute(own_1, "dir", swap) + (done_b[0, 0] + done_far[0, 0]))
    own_1, *around_0 = lax.optimization_barrier((own_1, *around_0))
    held_0 = both_cores([own_0, *around_0])
    around_1 = others(own_1)
    blocks = (blocks_a, blocks_b, blocks_u, blocks_v)


    def to_owner(mine, away, zero):
        came = [lax.ppermute(part, AXES, turn) for part, turn in zip(away, first_turn)]
        mine, *away = [mine[k] + came[0][k] + came[1][k] + came[2][k] for k in range(4)]
        came = [lax.ppermute(part, AXES, turn) for part, turn in zip(away, second_turn)]
        return mine + (came[0] + zero) + came[1] + came[2]

    mine, *away, done_0 = apply_blocks(table, held_0, blocks, 0)
    *around_1, done_0 = lax.optimization_barrier((*around_1, done_0))
    results = [to_owner(mine, away, done_0[0, 0])]
    mine, *away, done_1 = apply_blocks(table, both_cores([own_1, *around_1]), blocks, 1)
    results.append(to_owner(mine, away, done_1[0, 0]))
    parts = [r[:, :HALF] for r in results] + [r[:, HALF:] for r in results]
    return jnp.concatenate(parts, axis=1)


def solution(mesh):
    finer = Mesh(mesh.devices.reshape(SIZES), AXES)
    blocks = P(None, AXES, None, None)
    in_specs = (
        P("dir", None),
        P(None, ("y", "zhi", "x", "core"), "dir"),
        blocks,
        P(AXES, None),
        blocks,
        blocks,
        P(AXES, None),
        P(AXES),
        P(AXES, None),
    )
    out_specs = P(("x", "core", "dir", "y", "zhi"), None)
    return jax.shard_map(shards, mesh=finer, in_specs=in_specs, out_specs=out_specs, check_vma=False)
```

```python
import functools

import jax
import jax.numpy as jnp
from jax import lax
from jax.experimental import pallas as pl
from jax.experimental.pallas import tpu as pltpu
from jax.sharding import Mesh
from jax.sharding import PartitionSpec as P

AXES = ("dir", "y", "zhi", "x", "core")
ROW = ("y", "zhi")
COL = ("x", "core")
SIZES = (2, 4, 2, 4, 2)
CHUNKS = 2
CLUSTER = 512
HALF = 128
WIDE = 2 * HALF
PAD = 128
NEAR = 8
FAR = 4
VMEM_LIMIT = 60 << 20
SCOPED = 14 << 20

ANY = pl.BlockSpec(memory_space=pl.ANY)
SMEM = pl.BlockSpec(memory_space=pltpu.SMEM)
VMEM = pl.BlockSpec(memory_space=pltpu.VMEM)
HBM = pl.BlockSpec(memory_space=pltpu.HBM)
TOKEN = jax.ShapeDtypeStruct((8, 128), jnp.float32)

N_NEAR, N_FAR, NEAR_A, NEAR_B, FAR_A, FAR_B, RANK, ORDER, CORE, X = 0, 1, 2, 10, 18, 22, 26, 30, 46, 47


def split(values):
    high = values.astype(jnp.bfloat16)
    low = (values - high.astype(jnp.float32)).astype(jnp.bfloat16)
    return high, low


def dot(left, right):
    return jnp.dot(left, right, preferred_element_type=jnp.float32)


def rotations():
    tables = []
    for first in (True, False):
        for shift in (1, 2, 3):
            pairs = []
            for lo in range(2):
                for y in range(4):
                    for hi in range(2):
                        for x in range(4):
                            for core in range(2):
                                z = hi * 2 + lo
                                if (core == 0) == first:
                                    to_y, to_z = (y + shift) % 4, z
                                else:
                                    to_y, to_z = y, (z + shift) % 4
                                here = (((lo * 4 + y) * 2 + hi) * 4 + x) * 2 + core
                                there = (((to_z % 2 * 4 + to_y) * 2 + to_z // 2) * 4 + x) * 2 + core
                                pairs.append((here, there))
            tables.append(pairs)
    return tables[:3], tables[3:]


def rhs_kernel(cot_ref, rad_ref, out_0, out_1, cot, rad, sem_c, sem_r):
    width = cot.shape[1] // 2
    rows = rad.shape[1] // sem_r.shape[0]
    copies = [pltpu.make_async_copy(cot_ref, cot, sem_c.at[0])]
    for i in range(sem_r.shape[0]):
        tile = pl.ds(i * rows, rows)
        copies.append(pltpu.make_async_copy(rad_ref.at[:, tile], rad.at[:, tile], sem_r.at[i]))
    for copy in copies:
        copy.start()
    copies[0].wait()
    for i, copy in enumerate(copies[1:]):
        tile = slice(i * rows, (i + 1) * rows)
        copy.wait()
        for chunk, out_ref in enumerate((out_0, out_1)):
            re = cot[:, chunk * HALF : (chunk + 1) * HALF]
            im = cot[:, width + chunk * HALF : width + (chunk + 1) * HALF]
            out_ref[tile] = dot(rad[0, tile], jnp.concatenate([re, im], 1)) + dot(
                rad[1, tile], jnp.concatenate([-im, re], 1)
            )


def partial_rhs(cotangent, radiation):
    rows = radiation.shape[1]
    return pl.pallas_call(
        rhs_kernel,
        name="rhs",
        in_specs=[HBM, HBM],
        out_specs=[VMEM] * CHUNKS,
        out_shape=[pltpu.VMEM((rows, WIDE), jnp.float32)] * CHUNKS,
        scratch_shapes=[
            pltpu.VMEM(cotangent.shape, cotangent.dtype),
            pltpu.VMEM(radiation.shape, radiation.dtype),
            pltpu.SemaphoreType.DMA((1,)),
            pltpu.SemaphoreType.DMA((2,)),
        ],
        compiler_params=pltpu.CompilerParams(vmem_limit_bytes=SCOPED),
        cost_estimate=pl.CostEstimate(flops=1 << 30, bytes_accessed=4 << 20, transcendentals=0),
    )(*(pltpu.with_memory_space_constraint(f, pltpu.HBM) for f in (cotangent, radiation)))


def prepare_near_kernel(first, table, z_ref, out_ref, token, z_in, sem_in):
    slots, buffers = out_ref.shape[0], z_in.shape[0]
    token[...] = jnp.zeros_like(token)
    live = jnp.clip(table[N_NEAR] - first, 0, slots)

    def fetch(s):
        b = lax.rem(s, buffers)
        return pltpu.make_async_copy(z_ref.at[:, first + s], z_in.at[b], sem_in.at[b])

    for ahead in range(buffers - 1):

        @pl.when(ahead < live)
        def _():
            fetch(ahead).start()

    def near_step(s, _):
        @pl.when(s + buffers - 1 < live)
        def _():
            fetch(s + buffers - 1).start()

        fetch(s).wait()
        for part in range(2):
            high, low = split(z_in[lax.rem(s, buffers), part].T)
            out_ref[s, :, part * CLUSTER : (part + 1) * CLUSTER] = high
            out_ref[s, :, (part + 2) * CLUSTER : (part + 3) * CLUSTER] = low
        return 0

    lax.fori_loop(0, live, near_step, 0)


def prepare_near(table, near_z, first, slots):
    buffers = 3
    return pl.pallas_call(
        functools.partial(prepare_near_kernel, first),
        name=f"prepare_near_{first}",
        in_specs=[SMEM, HBM],
        out_specs=[VMEM, VMEM],
        out_shape=[pltpu.VMEM((slots, CLUSTER, 4 * CLUSTER), jnp.bfloat16), TOKEN],
        scratch_shapes=[
            pltpu.VMEM((buffers, 2, CLUSTER, CLUSTER), jnp.float32),
            pltpu.SemaphoreType.DMA((buffers,)),
        ],
        compiler_params=pltpu.CompilerParams(vmem_limit_bytes=SCOPED),
        cost_estimate=pl.CostEstimate(flops=1 << 28, bytes_accessed=slots << 21, transcendentals=0),
    )(table, pltpu.with_memory_space_constraint(near_z, pltpu.HBM))


def prepare_far_kernel(table, u_ref, v_ref, u_out, v_out, token, u_in, v_in, sem_u, sem_v):
    token[...] = jnp.zeros_like(token)
    far, rank_most = table[N_FAR], u_in.shape[2]

    def fetch(s):
        return (
            pltpu.make_async_copy(u_ref.at[:, s], u_in.at[s], sem_u.at[s]),
            pltpu.make_async_copy(v_ref.at[:, s], v_in.at[s], sem_v.at[s]),
        )

    def start(s, _):
        for copy in fetch(s):
            copy.start()
        return 0

    lax.fori_loop(0, far, start, 0)

    def far_step(s, _):
        for copy in fetch(s):
            copy.wait()
        live = lax.broadcasted_iota(jnp.int32, (PAD, CLUSTER), 0) < table[RANK + s]
        fill = jnp.zeros((PAD - rank_most, CLUSTER), jnp.float32)
        for part in range(2):
            padded = jnp.concatenate([u_in[s, part], fill], 0)
            high, low = split(jnp.where(live, padded, 0.0))
            u_out[s, :, part * CLUSTER : (part + 1) * CLUSTER] = high
            u_out[s, :, (part + 2) * CLUSTER : (part + 3) * CLUSTER] = low
            padded = jnp.concatenate([v_in[s, part], fill], 0)
            high, low = split(padded.T)
            v_out[s, :, part * PAD : (part + 1) * PAD] = high
            v_out[s, :, (part + 2) * PAD : (part + 3) * PAD] = low
        return 0

    lax.fori_loop(0, far, far_step, 0)


def prepare_far(table, far_ut, far_vt):
    rank_most = far_ut.shape[2]
    return pl.pallas_call(
        prepare_far_kernel,
        name="prepare_far",
        in_specs=[SMEM, HBM, HBM],
        out_specs=[VMEM, VMEM, VMEM],
        out_shape=[
            pltpu.VMEM((FAR, PAD, 4 * CLUSTER), jnp.bfloat16),
            pltpu.VMEM((FAR, CLUSTER, 4 * PAD), jnp.bfloat16),
            TOKEN,
        ],
        scratch_shapes=[
            pltpu.VMEM((FAR, 2, rank_most, CLUSTER), jnp.float32),
            pltpu.VMEM((FAR, 2, rank_most, CLUSTER), jnp.float32),
            pltpu.SemaphoreType.DMA((FAR,)),
            pltpu.SemaphoreType.DMA((FAR,)),
        ],
        compiler_params=pltpu.CompilerParams(vmem_limit_bytes=SCOPED),
        cost_estimate=pl.CostEstimate(flops=1 << 28, bytes_accessed=4 << 20, transcendentals=0),
    )(table, *(pltpu.with_memory_space_constraint(f, pltpu.HBM) for f in (far_ut, far_vt)))


def parts_of(values):
    high, low = split(values)
    high = jnp.concatenate([high, jnp.concatenate([-high[:, HALF:], high[:, :HALF]], 1)], 0)
    low = jnp.concatenate([low, jnp.concatenate([-low[:, HALF:], low[:, :HALF]], 1)], 0)
    return high, low


def product(left, values):
    high, low = parts_of(values)
    return dot(left, jnp.concatenate([high, high], 0)) + dot(left[:, : left.shape[1] // 2], low)


def apply_kernel(pieces, table, *refs):
    held, refs = refs[: len(pieces)], refs[len(pieces) :]
    (za_ref, zb_ref, u_ref, v_ref), outs, (token, x_buf, fx_buf, sem_x, sem_fx) = refs[:4], refs[4:8], refs[8:]
    near, far = table[N_NEAR], table[N_FAR]
    slots = za_ref.shape[0]

    def fetch(cluster, buf, sem):
        steps = lax.rem(table[X] + 4 - cluster // 2, 4)
        other = jnp.where(lax.rem(cluster, 2) == table[CORE], 0, 1)
        for ref, (came, crossed, row) in zip(held, pieces):

            @pl.when((steps == came) & (other == crossed))
            def _():
                pltpu.make_async_copy(ref, buf.at[pl.ds(row, ref.shape[0])], sem).start()

    def fetched(buf, sem):
        pltpu.make_async_copy(held[0], buf, sem).wait()

    def add(cluster, term):
        for half in range(2):
            rows = CLUSTER // 2
            place = table[ORDER + cluster * 2 + half]
            for steps, out_ref in enumerate(outs):

                @pl.when(place // 4 == steps)
                def _():
                    out_ref[lax.rem(place, 4)] += term[half * rows : (half + 1) * rows]

    fetch(table[NEAR_A], x_buf.at[0], sem_x.at[0])

    def far_start(s, _):
        fetch(table[FAR_A + s], fx_buf.at[s], sem_fx.at[s])
        return 0

    lax.fori_loop(0, far, far_start, 0)
    for out_ref in (*outs, token):
        out_ref[...] = jnp.zeros_like(out_ref)

    def near_steps(z_ref, first, last):
        def near_step(s, _):
            b = lax.rem(s, 2)

            @pl.when(s + 1 < near)
            def _():
                fetch(table[NEAR_A + s + 1], x_buf.at[1 - b], sem_x.at[1 - b])

            fetched(x_buf.at[b], sem_x.at[b])
            add(table[NEAR_B + s], product(z_ref[s - first], x_buf[b]))
            return 0

        lax.fori_loop(first, last, near_step, 0)

    near_steps(za_ref, 0, jnp.minimum(near, slots))
    near_steps(zb_ref, slots, near)

    def far_step(s, _):
        fetched(fx_buf.at[s], sem_fx.at[s])
        add(table[FAR_B + s], product(v_ref[s], product(u_ref[s], fx_buf[s])))
        return 0

    lax.fori_loop(0, far, far_step, 0)


def apply_blocks(table, pieces, held, blocks, index):
    return pl.pallas_call(
        functools.partial(apply_kernel, pieces),
        name=f"apply_{index}",
        in_specs=[SMEM] + [ANY] * len(held) + [VMEM] * 4,
        out_specs=[VMEM] * 5,
        out_shape=[jax.ShapeDtypeStruct((4, CLUSTER // 2, WIDE), jnp.float32)] * 4 + [TOKEN],
        scratch_shapes=[
            pltpu.VMEM((2, CLUSTER, WIDE), jnp.float32),
            pltpu.VMEM((FAR, CLUSTER, WIDE), jnp.float32),
            pltpu.SemaphoreType.DMA((2,)),
            pltpu.SemaphoreType.DMA((FAR,)),
        ],
        compiler_params=pltpu.CompilerParams(vmem_limit_bytes=SCOPED),
        cost_estimate=pl.CostEstimate(flops=40 << 30, bytes_accessed=8 << 20, transcendentals=0),
    )(table, *held, *blocks)


def scalars(near_pairs, far_pairs, far_ranks, block_counts):
    row_base = lax.axis_index(ROW) * 8
    col_base = lax.axis_index(COL) * 8
    core = lax.axis_index("core")
    index = lax.iota(jnp.int32, 16)
    steps_y = (index // 2 - lax.axis_index("y")) % 4
    steps_z = (index % 2 * 2 + index // 8 - lax.axis_index("zhi") * 2 - lax.axis_index("dir")) % 4
    order = jnp.where(core == 0, steps_y * 4 + steps_z, steps_z * 4 + steps_y)
    pieces = [
        block_counts[0],
        near_pairs[:, 0] - row_base,
        near_pairs[:, 1] - col_base,
        far_pairs[:, 0] - row_base,
        far_pairs[:, 1] - col_base,
        far_ranks,
        order,
        core[None],
        lax.axis_index("x")[None],
    ]
    return jnp.concatenate(pieces).astype(jnp.int32)


def shards(cotangent, radiation, near_z, near_pairs, far_ut, far_vt, far_pairs, far_ranks, block_counts):
    table = scalars(near_pairs, far_pairs, far_ranks, block_counts)
    own_0, own_1 = partial_rhs(cotangent, radiation)
    swap = [(0, 1), (1, 0)]
    first_turn, second_turn = rotations()

    def step(part, k):
        return lax.ppermute(part, "x", [(i, (i + k) % 4) for i in range(4)])

    def both_cores(mine):
        return mine + [lax.ppermute(part, "core", swap) for part in mine]

    def on_both(places):
        return tuple((came, crossed, row) for crossed in range(2) for came, row in places)

    blocks_a, done_a = prepare_near(table, near_z, 0, NEAR // 2)
    own_0 = own_0 + (lax.ppermute(own_0, "dir", swap) + done_a[0, 0])
    own_0, own_1 = lax.optimization_barrier((own_0, own_1))
    left_0, right_0 = step(own_0, 1), step(own_0, 3)
    blocks_b, done_b = prepare_near(table, near_z, NEAR // 2, NEAR // 2)
    blocks_u, blocks_v, done_far = prepare_far(table, far_ut, far_vt)
    own_1 = own_1 + (lax.ppermute(own_1, "dir", swap) + (done_b[0, 0] + done_far[0, 0]))
    own_1, left_0, right_0 = lax.optimization_barrier((own_1, left_0, right_0))
    middle = CLUSTER // 2
    upper_0, lower_0 = step(left_0[:middle], 1), step(right_0[middle:], 3)
    left_1, right_1 = step(own_1, 1), step(own_1, 3)
    own_1, upper_0, lower_0 = lax.optimization_barrier((own_1, upper_0, lower_0))
    around_1 = [left_1, step(own_1, 2), right_1]
    held_0 = both_cores([own_0, left_0, right_0, upper_0, lower_0])
    places_0 = on_both([(0, 0), (1, 0), (3, 0), (2, 0), (2, middle)])
    places_1 = on_both([(0, 0), (1, 0), (2, 0), (3, 0)])
    blocks = (blocks_a, blocks_b, blocks_u, blocks_v)


    def to_owner(mine, away, zero):
        came = [lax.ppermute(part, AXES, turn) for part, turn in zip(away, first_turn)]
        mine, *away = [mine[k] + came[0][k] + came[1][k] + came[2][k] for k in range(4)]
        came = [lax.ppermute(part, AXES, turn) for part, turn in zip(away, second_turn)]
        return mine + (came[0] + zero) + came[1] + came[2]

    mine, *away, done_0 = apply_blocks(table, places_0, held_0, blocks, 0)
    *around_1, done_0 = lax.optimization_barrier((*around_1, done_0))
    results = [to_owner(mine, away, done_0[0, 0])]
    mine, *away, done_1 = apply_blocks(table, places_1, both_cores([own_1, *around_1]), blocks, 1)
    results.append(to_owner(mine, away, done_1[0, 0]))
    parts = [r[:, :HALF] for r in results] + [r[:, HALF:] for r in results]
    return jnp.concatenate(parts, axis=1)


def solution(mesh):
    finer = Mesh(mesh.devices.reshape(SIZES), AXES)
    blocks = P(None, AXES, None, None)
    in_specs = (
        P("dir", None),
        P(None, ("y", "zhi", "x", "core"), "dir"),
        blocks,
        P(AXES, None),
        blocks,
        blocks,
        P(AXES, None),
        P(AXES),
        P(AXES, None),
    )
    out_specs = P(("x", "core", "dir", "y", "zhi"), None)
    return jax.shard_map(shards, mesh=finer, in_specs=in_specs, out_specs=out_specs, check_vma=False)
```

```python
import functools

import jax
import jax.numpy as jnp
from jax import lax
from jax.experimental import pallas as pl
from jax.experimental.pallas import tpu as pltpu
from jax.sharding import Mesh
from jax.sharding import PartitionSpec as P

AXES = ("dir", "y", "zhi", "x", "core")
ROW = ("y", "zhi")
COL = ("x", "core")
SIZES = (2, 4, 2, 4, 2)
CHUNKS = 2
CLUSTER = 512
HALF = 128
WIDE = 2 * HALF
PAD = 128
NEAR = 8
FAR = 4
VMEM_LIMIT = 60 << 20
SCOPED = 14 << 20

ANY = pl.BlockSpec(memory_space=pl.ANY)
SMEM = pl.BlockSpec(memory_space=pltpu.SMEM)
VMEM = pl.BlockSpec(memory_space=pltpu.VMEM)
HBM = pl.BlockSpec(memory_space=pltpu.HBM)
TOKEN = jax.ShapeDtypeStruct((8, 128), jnp.float32)

N_NEAR, N_FAR, NEAR_A, NEAR_B, FAR_A, FAR_B, RANK, ORDER, CORE, X = 0, 1, 2, 10, 18, 22, 26, 30, 46, 47


def split(values):
    high = values.astype(jnp.bfloat16)
    low = (values - high.astype(jnp.float32)).astype(jnp.bfloat16)
    return high, low


def dot(left, right):
    return jnp.dot(left, right, preferred_element_type=jnp.float32)


def rotations():
    tables = []
    for first in (True, False):
        for shift in (1, 2, 3):
            pairs = []
            for lo in range(2):
                for y in range(4):
                    for hi in range(2):
                        for x in range(4):
                            for core in range(2):
                                z = hi * 2 + lo
                                if (core == 0) == first:
                                    to_y, to_z = (y + shift) % 4, z
                                else:
                                    to_y, to_z = y, (z + shift) % 4
                                here = (((lo * 4 + y) * 2 + hi) * 4 + x) * 2 + core
                                there = (((to_z % 2 * 4 + to_y) * 2 + to_z // 2) * 4 + x) * 2 + core
                                pairs.append((here, there))
            tables.append(pairs)
    return tables[:3], tables[3:]


def rhs_kernel(cot_ref, rad_ref, out_0, out_1, cot, rad, sem_c, sem_r):
    width = cot.shape[1] // 2
    rows = rad.shape[1] // sem_r.shape[0]
    copies = [pltpu.make_async_copy(cot_ref, cot, sem_c.at[0])]
    for i in range(sem_r.shape[0]):
        tile = pl.ds(i * rows, rows)
        copies.append(pltpu.make_async_copy(rad_ref.at[:, tile], rad.at[:, tile], sem_r.at[i]))
    for copy in copies:
        copy.start()
    copies[0].wait()
    for i, copy in enumerate(copies[1:]):
        tile = slice(i * rows, (i + 1) * rows)
        copy.wait()
        for chunk, out_ref in enumerate((out_0, out_1)):
            re = cot[:, chunk * HALF : (chunk + 1) * HALF]
            im = cot[:, width + chunk * HALF : width + (chunk + 1) * HALF]
            out_ref[tile] = dot(rad[0, tile], jnp.concatenate([re, im], 1)) + dot(
                rad[1, tile], jnp.concatenate([-im, re], 1)
            )


def partial_rhs(cotangent, radiation):
    rows = radiation.shape[1]
    return pl.pallas_call(
        rhs_kernel,
        name="rhs",
        in_specs=[HBM, HBM],
        out_specs=[VMEM] * CHUNKS,
        out_shape=[pltpu.VMEM((rows, WIDE), jnp.float32)] * CHUNKS,
        scratch_shapes=[
            pltpu.VMEM(cotangent.shape, cotangent.dtype),
            pltpu.VMEM(radiation.shape, radiation.dtype),
            pltpu.SemaphoreType.DMA((1,)),
            pltpu.SemaphoreType.DMA((2,)),
        ],
        compiler_params=pltpu.CompilerParams(vmem_limit_bytes=SCOPED),
        cost_estimate=pl.CostEstimate(flops=1 << 30, bytes_accessed=4 << 20, transcendentals=0),
    )(*(pltpu.with_memory_space_constraint(f, pltpu.HBM) for f in (cotangent, radiation)))


def prepare_near_kernel(first, table, z_ref, out_ref, token, z_in, sem_in):
    slots, buffers = out_ref.shape[0], z_in.shape[0]
    token[...] = jnp.zeros_like(token)
    live = jnp.clip(table[N_NEAR] - first, 0, slots)

    def fetch(s):
        b = lax.rem(s, buffers)
        return pltpu.make_async_copy(z_ref.at[:, first + s], z_in.at[b], sem_in.at[b])

    for ahead in range(buffers - 1):

        @pl.when(ahead < live)
        def _():
            fetch(ahead).start()

    def near_step(s, _):
        @pl.when(s + buffers - 1 < live)
        def _():
            fetch(s + buffers - 1).start()

        fetch(s).wait()
        for part in range(2):
            high, low = split(z_in[lax.rem(s, buffers), part].T)
            out_ref[s, :, part * CLUSTER : (part + 1) * CLUSTER] = high
            out_ref[s, :, (part + 2) * CLUSTER : (part + 3) * CLUSTER] = low
        return 0

    lax.fori_loop(0, live, near_step, 0)


def prepare_near(table, near_z, first, slots):
    buffers = 3
    return pl.pallas_call(
        functools.partial(prepare_near_kernel, first),
        name=f"prepare_near_{first}",
        in_specs=[SMEM, HBM],
        out_specs=[VMEM, VMEM],
        out_shape=[pltpu.VMEM((slots, CLUSTER, 4 * CLUSTER), jnp.bfloat16), TOKEN],
        scratch_shapes=[
            pltpu.VMEM((buffers, 2, CLUSTER, CLUSTER), jnp.float32),
            pltpu.SemaphoreType.DMA((buffers,)),
        ],
        compiler_params=pltpu.CompilerParams(vmem_limit_bytes=SCOPED),
        cost_estimate=pl.CostEstimate(flops=1 << 28, bytes_accessed=slots << 21, transcendentals=0),
    )(table, pltpu.with_memory_space_constraint(near_z, pltpu.HBM))


def prepare_far_kernel(table, u_ref, v_ref, u_out, v_out, token, u_in, v_in, sem_u, sem_v):
    token[...] = jnp.zeros_like(token)
    far, rank_most = table[N_FAR], u_in.shape[2]

    def fetch(s):
        return (
            pltpu.make_async_copy(u_ref.at[:, s], u_in.at[s], sem_u.at[s]),
            pltpu.make_async_copy(v_ref.at[:, s], v_in.at[s], sem_v.at[s]),
        )

    def start(s, _):
        for copy in fetch(s):
            copy.start()
        return 0

    lax.fori_loop(0, far, start, 0)

    def far_step(s, _):
        for copy in fetch(s):
            copy.wait()
        live = lax.broadcasted_iota(jnp.int32, (PAD, CLUSTER), 0) < table[RANK + s]
        fill = jnp.zeros((PAD - rank_most, CLUSTER), jnp.float32)
        for part in range(2):
            padded = jnp.concatenate([u_in[s, part], fill], 0)
            high, low = split(jnp.where(live, padded, 0.0))
            u_out[s, :, part * CLUSTER : (part + 1) * CLUSTER] = high
            u_out[s, :, (part + 2) * CLUSTER : (part + 3) * CLUSTER] = low
            padded = jnp.concatenate([v_in[s, part], fill], 0)
            high, low = split(padded.T)
            v_out[s, :, part * PAD : (part + 1) * PAD] = high
            v_out[s, :, (part + 2) * PAD : (part + 3) * PAD] = low
        return 0

    lax.fori_loop(0, far, far_step, 0)


def prepare_far(table, far_ut, far_vt):
    rank_most = far_ut.shape[2]
    return pl.pallas_call(
        prepare_far_kernel,
        name="prepare_far",
        in_specs=[SMEM, HBM, HBM],
        out_specs=[VMEM, VMEM, VMEM],
        out_shape=[
            pltpu.VMEM((FAR, PAD, 4 * CLUSTER), jnp.bfloat16),
            pltpu.VMEM((FAR, CLUSTER, 4 * PAD), jnp.bfloat16),
            TOKEN,
        ],
        scratch_shapes=[
            pltpu.VMEM((FAR, 2, rank_most, CLUSTER), jnp.float32),
            pltpu.VMEM((FAR, 2, rank_most, CLUSTER), jnp.float32),
            pltpu.SemaphoreType.DMA((FAR,)),
            pltpu.SemaphoreType.DMA((FAR,)),
        ],
        compiler_params=pltpu.CompilerParams(vmem_limit_bytes=SCOPED),
        cost_estimate=pl.CostEstimate(flops=1 << 28, bytes_accessed=4 << 20, transcendentals=0),
    )(table, *(pltpu.with_memory_space_constraint(f, pltpu.HBM) for f in (far_ut, far_vt)))


def parts_of(values):
    high, low = split(values)
    high = jnp.concatenate([high, jnp.concatenate([-high[:, HALF:], high[:, :HALF]], 1)], 0)
    low = jnp.concatenate([low, jnp.concatenate([-low[:, HALF:], low[:, :HALF]], 1)], 0)
    return high, low


def product(left, values):
    high, low = parts_of(values)
    return dot(left, jnp.concatenate([high, high], 0)) + dot(left[:, : left.shape[1] // 2], low)


def pack_kernel(*refs):
    parts, out_ref, sem = refs[:-2], refs[-2], refs[-1]
    copies, first = [], 0
    for i, part in enumerate(parts):
        rows = part.shape[0]
        copies.append(pltpu.make_async_copy(part, out_ref.at[pl.ds(first, rows)], sem.at[i]))
        first += rows
    for copy in copies:
        copy.start()
    for copy in copies:
        copy.wait()


def pack(parts, index):
    rows = sum(part.shape[0] for part in parts)
    return pl.pallas_call(
        pack_kernel,
        name=f"pack_{index}",
        in_specs=[ANY] * len(parts),
        out_specs=ANY,
        out_shape=jax.ShapeDtypeStruct((rows, parts[0].shape[1]), jnp.float32),
        scratch_shapes=[pltpu.SemaphoreType.DMA((len(parts),))],
        compiler_params=pltpu.CompilerParams(vmem_limit_bytes=SCOPED),
        cost_estimate=pl.CostEstimate(flops=0, bytes_accessed=4 << 20, transcendentals=0),
    )(*parts)


def apply_kernel(table, *refs):
    held, (za_ref, zb_ref, u_ref, v_ref) = refs[:2], refs[2:6]
    outs, (token, x_buf, fx_buf, sem_x, sem_fx) = refs[6:10], refs[10:]
    near, far = table[N_NEAR], table[N_FAR]
    slots = za_ref.shape[0]

    def fetch(cluster, buf, sem):
        steps = lax.rem(table[X] + 4 - cluster // 2, 4)
        rows = pl.ds(pl.multiple_of(steps * CLUSTER, CLUSTER), CLUSTER)
        own_core = lax.rem(cluster, 2) == table[CORE]
        for ref, here in zip(held, (own_core, jnp.logical_not(own_core))):

            @pl.when(here)
            def _():
                pltpu.make_async_copy(ref.at[rows], buf, sem).start()

    def fetched(buf, sem):
        pltpu.make_async_copy(held[0].at[pl.ds(0, CLUSTER)], buf, sem).wait()

    def add(cluster, term):
        for half in range(2):
            rows = CLUSTER // 2
            place = table[ORDER + cluster * 2 + half]
            for steps, out_ref in enumerate(outs):

                @pl.when(place // 4 == steps)
                def _():
                    out_ref[lax.rem(place, 4)] += term[half * rows : (half + 1) * rows]

    fetch(table[NEAR_A], x_buf.at[0], sem_x.at[0])

    def far_start(s, _):
        fetch(table[FAR_A + s], fx_buf.at[s], sem_fx.at[s])
        return 0

    lax.fori_loop(0, far, far_start, 0)
    for out_ref in (*outs, token):
        out_ref[...] = jnp.zeros_like(out_ref)

    def near_steps(z_ref, first, last):
        def near_step(s, _):
            b = lax.rem(s, 2)

            @pl.when(s + 1 < near)
            def _():
                fetch(table[NEAR_A + s + 1], x_buf.at[1 - b], sem_x.at[1 - b])

            fetched(x_buf.at[b], sem_x.at[b])
            add(table[NEAR_B + s], product(z_ref[s - first], x_buf[b]))
            return 0

        lax.fori_loop(first, last, near_step, 0)

    near_steps(za_ref, 0, jnp.minimum(near, slots))
    near_steps(zb_ref, slots, near)

    def far_step(s, _):
        fetched(fx_buf.at[s], sem_fx.at[s])
        add(table[FAR_B + s], product(v_ref[s], product(u_ref[s], fx_buf[s])))
        return 0

    lax.fori_loop(0, far, far_step, 0)


def apply_blocks(table, held, blocks, index):
    return pl.pallas_call(
        apply_kernel,
        name=f"apply_{index}",
        in_specs=[SMEM] + [ANY] * 2 + [VMEM] * 4,
        out_specs=[VMEM] * 5,
        out_shape=[jax.ShapeDtypeStruct((4, CLUSTER // 2, WIDE), jnp.float32)] * 4 + [TOKEN],
        scratch_shapes=[
            pltpu.VMEM((2, CLUSTER, WIDE), jnp.float32),
            pltpu.VMEM((FAR, CLUSTER, WIDE), jnp.float32),
            pltpu.SemaphoreType.DMA((2,)),
            pltpu.SemaphoreType.DMA((FAR,)),
        ],
        compiler_params=pltpu.CompilerParams(vmem_limit_bytes=SCOPED),
        cost_estimate=pl.CostEstimate(flops=40 << 30, bytes_accessed=8 << 20, transcendentals=0),
    )(table, *held, *blocks)


def scalars(near_pairs, far_pairs, far_ranks, block_counts):
    row_base = lax.axis_index(ROW) * 8
    col_base = lax.axis_index(COL) * 8
    core = lax.axis_index("core")
    index = lax.iota(jnp.int32, 16)
    steps_y = (index // 2 - lax.axis_index("y")) % 4
    steps_z = (index % 2 * 2 + index // 8 - lax.axis_index("zhi") * 2 - lax.axis_index("dir")) % 4
    order = jnp.where(core == 0, steps_y * 4 + steps_z, steps_z * 4 + steps_y)
    pieces = [
        block_counts[0],
        near_pairs[:, 0] - row_base,
        near_pairs[:, 1] - col_base,
        far_pairs[:, 0] - row_base,
        far_pairs[:, 1] - col_base,
        far_ranks,
        order,
        core[None],
        lax.axis_index("x")[None],
    ]
    return jnp.concatenate(pieces).astype(jnp.int32)


def shards(cotangent, radiation, near_z, near_pairs, far_ut, far_vt, far_pairs, far_ranks, block_counts):
    table = scalars(near_pairs, far_pairs, far_ranks, block_counts)
    own_0, own_1 = partial_rhs(cotangent, radiation)
    swap = [(0, 1), (1, 0)]
    first_turn, second_turn = rotations()

    def step(part, k):
        return lax.ppermute(part, "x", [(i, (i + k) % 4) for i in range(4)])

    def both_cores(parts, index):
        mine = pack(parts, index)
        return mine, lax.ppermute(mine, "core", swap)

    blocks_a, done_a = prepare_near(table, near_z, 0, NEAR // 2)
    own_0 = own_0 + (lax.ppermute(own_0, "dir", swap) + done_a[0, 0])
    own_0, own_1 = lax.optimization_barrier((own_0, own_1))
    left_0, right_0 = step(own_0, 1), step(own_0, 3)
    blocks_b, done_b = prepare_near(table, near_z, NEAR // 2, NEAR // 2)
    blocks_u, blocks_v, done_far = prepare_far(table, far_ut, far_vt)
    own_1 = own_1 + (lax.ppermute(own_1, "dir", swap) + (done_b[0, 0] + done_far[0, 0]))
    own_1, left_0, right_0 = lax.optimization_barrier((own_1, left_0, right_0))
    middle = CLUSTER // 2
    upper_0, lower_0 = step(left_0[:middle], 1), step(right_0[middle:], 3)
    left_1, right_1 = step(own_1, 1), step(own_1, 3)
    own_1, upper_0, lower_0 = lax.optimization_barrier((own_1, upper_0, lower_0))
    across_1 = step(own_1, 2)
    held_0 = both_cores([own_0, left_0, upper_0, lower_0, right_0], 0)
    blocks = (blocks_a, blocks_b, blocks_u, blocks_v)


    def to_owner(mine, away, zero):
        came = [lax.ppermute(part, AXES, turn) for part, turn in zip(away, first_turn)]
        mine, *away = [mine[k] + came[0][k] + came[1][k] + came[2][k] for k in range(4)]
        came = [lax.ppermute(part, AXES, turn) for part, turn in zip(away, second_turn)]
        return mine + (came[0] + zero) + came[1] + came[2]

    mine, *away, done_0 = apply_blocks(table, held_0, blocks, 0)
    *parts_1, done_0 = lax.optimization_barrier((own_1, left_1, across_1, right_1, done_0))
    results = [to_owner(mine, away, done_0[0, 0])]
    mine, *away, done_1 = apply_blocks(table, both_cores(parts_1, 1), blocks, 1)
    results.append(to_owner(mine, away, done_1[0, 0]))
    parts = [r[:, :HALF] for r in results] + [r[:, HALF:] for r in results]
    return jnp.concatenate(parts, axis=1)


def solution(mesh):
    finer = Mesh(mesh.devices.reshape(SIZES), AXES)
    blocks = P(None, AXES, None, None)
    in_specs = (
        P("dir", None),
        P(None, ("y", "zhi", "x", "core"), "dir"),
        blocks,
        P(AXES, None),
        blocks,
        blocks,
        P(AXES, None),
        P(AXES),
        P(AXES, None),
    )
    out_specs = P(("x", "core", "dir", "y", "zhi"), None)
    return jax.shard_map(shards, mesh=finer, in_specs=in_specs, out_specs=out_specs, check_vma=False)
```

```python
import functools

import jax
import jax.numpy as jnp
from jax import lax
from jax.experimental import pallas as pl
from jax.experimental.pallas import tpu as pltpu
from jax.sharding import Mesh
from jax.sharding import PartitionSpec as P

AXES = ("dir", "y", "zhi", "x", "core")
ROW = ("y", "zhi")
COL = ("x", "core")
SIZES = (2, 4, 2, 4, 2)
CHUNKS = 2
COST = (40 << 30, 40 << 30)
CLUSTER = 512
HALF = 128
WIDE = 2 * HALF
PAD = 128
NEAR = 8
FAR = 4
VMEM_LIMIT = 60 << 20
SCOPED = 14 << 20

ANY = pl.BlockSpec(memory_space=pl.ANY)
SMEM = pl.BlockSpec(memory_space=pltpu.SMEM)
VMEM = pl.BlockSpec(memory_space=pltpu.VMEM)
HBM = pl.BlockSpec(memory_space=pltpu.HBM)
TOKEN = jax.ShapeDtypeStruct((8, 128), jnp.float32)

N_NEAR, N_FAR, NEAR_A, NEAR_B, FAR_A, FAR_B, RANK, ORDER, CORE, X = 0, 1, 2, 10, 18, 22, 26, 30, 46, 47


def split(values):
    high = values.astype(jnp.bfloat16)
    low = (values - high.astype(jnp.float32)).astype(jnp.bfloat16)
    return high, low


def dot(left, right):
    return jnp.dot(left, right, preferred_element_type=jnp.float32)


def rotations():
    tables = []
    for first in (True, False):
        for shift in (1, 2, 3):
            pairs = []
            for lo in range(2):
                for y in range(4):
                    for hi in range(2):
                        for x in range(4):
                            for core in range(2):
                                z = hi * 2 + lo
                                if (core == 0) == first:
                                    to_y, to_z = (y + shift) % 4, z
                                else:
                                    to_y, to_z = y, (z + shift) % 4
                                here = (((lo * 4 + y) * 2 + hi) * 4 + x) * 2 + core
                                there = (((to_z % 2 * 4 + to_y) * 2 + to_z // 2) * 4 + x) * 2 + core
                                pairs.append((here, there))
            tables.append(pairs)
    return tables[:3], tables[3:]


def rhs_kernel(cot_ref, rad_ref, out_0, out_1, cot, rad, sem_c, sem_r):
    width = cot.shape[1] // 2
    rows = rad.shape[1] // sem_r.shape[0]
    copies = [pltpu.make_async_copy(cot_ref, cot, sem_c.at[0])]
    for i in range(sem_r.shape[0]):
        tile = pl.ds(i * rows, rows)
        copies.append(pltpu.make_async_copy(rad_ref.at[:, tile], rad.at[:, tile], sem_r.at[i]))
    for copy in copies:
        copy.start()
    copies[0].wait()
    for i, copy in enumerate(copies[1:]):
        tile = slice(i * rows, (i + 1) * rows)
        copy.wait()
        for chunk, out_ref in enumerate((out_0, out_1)):
            re = cot[:, chunk * HALF : (chunk + 1) * HALF]
            im = cot[:, width + chunk * HALF : width + (chunk + 1) * HALF]
            out_ref[tile] = dot(rad[0, tile], jnp.concatenate([re, im], 1)) + dot(
                rad[1, tile], jnp.concatenate([-im, re], 1)
            )


def partial_rhs(cotangent, radiation):
    rows = radiation.shape[1]
    return pl.pallas_call(
        rhs_kernel,
        name="rhs",
        in_specs=[HBM, HBM],
        out_specs=[VMEM] * CHUNKS,
        out_shape=[pltpu.VMEM((rows, WIDE), jnp.float32)] * CHUNKS,
        scratch_shapes=[
            pltpu.VMEM(cotangent.shape, cotangent.dtype),
            pltpu.VMEM(radiation.shape, radiation.dtype),
            pltpu.SemaphoreType.DMA((1,)),
            pltpu.SemaphoreType.DMA((2,)),
        ],
        compiler_params=pltpu.CompilerParams(vmem_limit_bytes=SCOPED),
        cost_estimate=pl.CostEstimate(flops=1 << 30, bytes_accessed=4 << 20, transcendentals=0),
    )(*(pltpu.with_memory_space_constraint(f, pltpu.HBM) for f in (cotangent, radiation)))


def prepare_near_kernel(first, table, z_ref, out_ref, token, z_in, sem_in):
    slots, buffers = out_ref.shape[0], z_in.shape[0]
    token[...] = jnp.zeros_like(token)
    live = jnp.clip(table[N_NEAR] - first, 0, slots)

    def fetch(s):
        b = lax.rem(s, buffers)
        return pltpu.make_async_copy(z_ref.at[:, first + s], z_in.at[b], sem_in.at[b])

    for ahead in range(buffers - 1):

        @pl.when(ahead < live)
        def _():
            fetch(ahead).start()

    def near_step(s, _):
        @pl.when(s + buffers - 1 < live)
        def _():
            fetch(s + buffers - 1).start()

        fetch(s).wait()
        for part in range(2):
            high, low = split(z_in[lax.rem(s, buffers), part].T)
            out_ref[s, :, part * CLUSTER : (part + 1) * CLUSTER] = high
            out_ref[s, :, (part + 2) * CLUSTER : (part + 3) * CLUSTER] = low
        return 0

    lax.fori_loop(0, live, near_step, 0)


def prepare_near(table, near_z, first, slots):
    buffers = 3
    return pl.pallas_call(
        functools.partial(prepare_near_kernel, first),
        name=f"prepare_near_{first}",
        in_specs=[SMEM, HBM],
        out_specs=[VMEM, VMEM],
        out_shape=[pltpu.VMEM((slots, CLUSTER, 4 * CLUSTER), jnp.bfloat16), TOKEN],
        scratch_shapes=[
            pltpu.VMEM((buffers, 2, CLUSTER, CLUSTER), jnp.float32),
            pltpu.SemaphoreType.DMA((buffers,)),
        ],
        compiler_params=pltpu.CompilerParams(vmem_limit_bytes=SCOPED),
        cost_estimate=pl.CostEstimate(flops=1 << 28, bytes_accessed=slots << 21, transcendentals=0),
    )(table, pltpu.with_memory_space_constraint(near_z, pltpu.HBM))


def prepare_far_kernel(table, u_ref, v_ref, u_out, v_out, token, u_in, v_in, sem_u, sem_v):
    token[...] = jnp.zeros_like(token)
    far, rank_most = table[N_FAR], u_in.shape[2]

    def fetch(s):
        return (
            pltpu.make_async_copy(u_ref.at[:, s], u_in.at[s], sem_u.at[s]),
            pltpu.make_async_copy(v_ref.at[:, s], v_in.at[s], sem_v.at[s]),
        )

    def start(s, _):
        for copy in fetch(s):
            copy.start()
        return 0

    lax.fori_loop(0, far, start, 0)

    def far_step(s, _):
        for copy in fetch(s):
            copy.wait()
        live = lax.broadcasted_iota(jnp.int32, (PAD, CLUSTER), 0) < table[RANK + s]
        fill = jnp.zeros((PAD - rank_most, CLUSTER), jnp.float32)
        for part in range(2):
            padded = jnp.concatenate([u_in[s, part], fill], 0)
            high, low = split(jnp.where(live, padded, 0.0))
            u_out[s, :, part * CLUSTER : (part + 1) * CLUSTER] = high
            u_out[s, :, (part + 2) * CLUSTER : (part + 3) * CLUSTER] = low
            padded = jnp.concatenate([v_in[s, part], fill], 0)
            high, low = split(padded.T)
            v_out[s, :, part * PAD : (part + 1) * PAD] = high
            v_out[s, :, (part + 2) * PAD : (part + 3) * PAD] = low
        return 0

    lax.fori_loop(0, far, far_step, 0)


def prepare_far(table, far_ut, far_vt):
    rank_most = far_ut.shape[2]
    return pl.pallas_call(
        prepare_far_kernel,
        name="prepare_far",
        in_specs=[SMEM, HBM, HBM],
        out_specs=[VMEM, VMEM, VMEM],
        out_shape=[
            pltpu.VMEM((FAR, PAD, 4 * CLUSTER), jnp.bfloat16),
            pltpu.VMEM((FAR, CLUSTER, 4 * PAD), jnp.bfloat16),
            TOKEN,
        ],
        scratch_shapes=[
            pltpu.VMEM((FAR, 2, rank_most, CLUSTER), jnp.float32),
            pltpu.VMEM((FAR, 2, rank_most, CLUSTER), jnp.float32),
            pltpu.SemaphoreType.DMA((FAR,)),
            pltpu.SemaphoreType.DMA((FAR,)),
        ],
        compiler_params=pltpu.CompilerParams(vmem_limit_bytes=SCOPED),
        cost_estimate=pl.CostEstimate(flops=1 << 28, bytes_accessed=4 << 20, transcendentals=0),
    )(table, *(pltpu.with_memory_space_constraint(f, pltpu.HBM) for f in (far_ut, far_vt)))


def parts_of(values):
    high, low = split(values)
    high = jnp.concatenate([high, jnp.concatenate([-high[:, HALF:], high[:, :HALF]], 1)], 0)
    low = jnp.concatenate([low, jnp.concatenate([-low[:, HALF:], low[:, :HALF]], 1)], 0)
    return high, low


def product(left, values):
    high, low = parts_of(values)
    return dot(left, jnp.concatenate([high, high], 0)) + dot(left[:, : left.shape[1] // 2], low)


def pack_kernel(*refs):
    parts, out_ref, sem = refs[:-2], refs[-2], refs[-1]
    copies, first = [], 0
    for i, part in enumerate(parts):
        rows = part.shape[0]
        copies.append(pltpu.make_async_copy(part, out_ref.at[pl.ds(first, rows)], sem.at[i]))
        first += rows
    for copy in copies:
        copy.start()
    for copy in copies:
        copy.wait()


def pack(parts, index):
    rows = sum(part.shape[0] for part in parts)
    return pl.pallas_call(
        pack_kernel,
        name=f"pack_{index}",
        in_specs=[ANY] * len(parts),
        out_specs=ANY,
        out_shape=jax.ShapeDtypeStruct((rows, parts[0].shape[1]), jnp.float32),
        scratch_shapes=[pltpu.SemaphoreType.DMA((len(parts),))],
        compiler_params=pltpu.CompilerParams(vmem_limit_bytes=SCOPED),
        cost_estimate=pl.CostEstimate(flops=0, bytes_accessed=4 << 20, transcendentals=0),
    )(*parts)


def apply_kernel(table, *refs):
    held, (za_ref, zb_ref, u_ref, v_ref) = refs[:2], refs[2:6]
    outs, (token, x_buf, fx_buf, sem_x, sem_fx) = refs[6:10], refs[10:]
    near, far = table[N_NEAR], table[N_FAR]
    slots = za_ref.shape[0]

    def fetch(cluster, buf, sem):
        steps = lax.rem(table[X] + 4 - cluster // 2, 4)
        rows = pl.ds(pl.multiple_of(steps * CLUSTER, CLUSTER), CLUSTER)
        own_core = lax.rem(cluster, 2) == table[CORE]
        for ref, here in zip(held, (own_core, jnp.logical_not(own_core))):

            @pl.when(here)
            def _():
                pltpu.make_async_copy(ref.at[rows], buf, sem).start()

    def fetched(buf, sem):
        pltpu.make_async_copy(held[0].at[pl.ds(0, CLUSTER)], buf, sem).wait()

    def add(cluster, term):
        for half in range(2):
            rows = CLUSTER // 2
            place = table[ORDER + cluster * 2 + half]
            for steps, out_ref in enumerate(outs):

                @pl.when(place // 4 == steps)
                def _():
                    out_ref[lax.rem(place, 4)] += term[half * rows : (half + 1) * rows]

    fetch(table[NEAR_A], x_buf.at[0], sem_x.at[0])

    def far_start(s, _):
        fetch(table[FAR_A + s], fx_buf.at[s], sem_fx.at[s])
        return 0

    lax.fori_loop(0, far, far_start, 0)
    for out_ref in (*outs, token):
        out_ref[...] = jnp.zeros_like(out_ref)

    def near_steps(z_ref, first, last):
        def near_step(s, _):
            b = lax.rem(s, 2)

            @pl.when(s + 1 < near)
            def _():
                fetch(table[NEAR_A + s + 1], x_buf.at[1 - b], sem_x.at[1 - b])

            fetched(x_buf.at[b], sem_x.at[b])
            add(table[NEAR_B + s], product(z_ref[s - first], x_buf[b]))
            return 0

        lax.fori_loop(first, last, near_step, 0)

    near_steps(za_ref, 0, jnp.minimum(near, slots))
    near_steps(zb_ref, slots, near)

    def far_step(s, _):
        fetched(fx_buf.at[s], sem_fx.at[s])
        add(table[FAR_B + s], product(v_ref[s], product(u_ref[s], fx_buf[s])))
        return 0

    lax.fori_loop(0, far, far_step, 0)


def apply_blocks(table, held, blocks, index):
    return pl.pallas_call(
        apply_kernel,
        name=f"apply_{index}",
        in_specs=[SMEM] + [ANY] * 2 + [VMEM] * 4,
        out_specs=[VMEM] * 5,
        out_shape=[jax.ShapeDtypeStruct((4, CLUSTER // 2, WIDE), jnp.float32)] * 4 + [TOKEN],
        scratch_shapes=[
            pltpu.VMEM((2, CLUSTER, WIDE), jnp.float32),
            pltpu.VMEM((FAR, CLUSTER, WIDE), jnp.float32),
            pltpu.SemaphoreType.DMA((2,)),
            pltpu.SemaphoreType.DMA((FAR,)),
        ],
        compiler_params=pltpu.CompilerParams(vmem_limit_bytes=SCOPED),
        cost_estimate=pl.CostEstimate(flops=COST[index], bytes_accessed=1, transcendentals=0),
    )(table, *held, *blocks)


def scalars(near_pairs, far_pairs, far_ranks, block_counts):
    row_base = lax.axis_index(ROW) * 8
    col_base = lax.axis_index(COL) * 8
    core = lax.axis_index("core")
    index = lax.iota(jnp.int32, 16)
    steps_y = (index // 2 - lax.axis_index("y")) % 4
    steps_z = (index % 2 * 2 + index // 8 - lax.axis_index("zhi") * 2 - lax.axis_index("dir")) % 4
    order = jnp.where(core == 0, steps_y * 4 + steps_z, steps_z * 4 + steps_y)
    pieces = [
        block_counts[0],
        near_pairs[:, 0] - row_base,
        near_pairs[:, 1] - col_base,
        far_pairs[:, 0] - row_base,
        far_pairs[:, 1] - col_base,
        far_ranks,
        order,
        core[None],
        lax.axis_index("x")[None],
    ]
    return jnp.concatenate(pieces).astype(jnp.int32)


def shards(cotangent, radiation, near_z, near_pairs, far_ut, far_vt, far_pairs, far_ranks, block_counts):
    table = scalars(near_pairs, far_pairs, far_ranks, block_counts)
    own_0, own_1 = partial_rhs(cotangent, radiation)
    swap = [(0, 1), (1, 0)]
    first_turn, second_turn = rotations()

    def across_dir(part, name):
        with jax.named_scope(name):
            return lax.ppermute(part, "dir", swap)

    def step(part, k, name):
        with jax.named_scope(name):
            return lax.ppermute(part, "x", [(i, (i + k) % 4) for i in range(4)])

    def both_cores(parts, index):
        mine = pack(parts, index)
        with jax.named_scope(f"P_S{index}"):
            return mine, lax.ppermute(mine, "core", swap)

    middle = CLUSTER // 2
    blocks_a, done_a = prepare_near(table, near_z, 0, NEAR // 2)
    upper, lower = own_0[:middle], own_0[middle:]
    upper = upper + (across_dir(upper, "P_ZU") + done_a[0, 0])
    blocks_b, done_b = prepare_near(table, near_z, NEAR // 2, NEAR // 2)
    blocks_u, blocks_v, done_far = prepare_far(table, far_ut, far_vt)
    upper, lower = lax.optimization_barrier((upper, lower))
    left_u, right_u = step(upper, 1, "P_LU"), step(upper, 3, "P_RU")
    lower = lower + (across_dir(lower, "P_ZL") + done_b[0, 0])
    own_1, lower, left_u, right_u = lax.optimization_barrier((own_1, lower, left_u, right_u))
    left_l, right_l = step(lower, 1, "P_LL"), step(lower, 3, "P_RL")
    own_1 = own_1 + (across_dir(own_1, "P_Z1") + done_far[0, 0])
    upper_0, lower_0 = step(left_u, 1, "P_A0"), step(right_l, 3, "P_B0")
    own_1, upper_0, lower_0 = lax.optimization_barrier((own_1, upper_0, lower_0))
    left_1, right_1 = step(own_1, 1, "P_L1"), step(own_1, 3, "P_R1")
    across_1 = step(own_1, 2, "P_K1")
    held_0 = both_cores([upper, lower, left_u, left_l, upper_0, lower_0, right_u, right_l], 0)
    blocks = (blocks_a, blocks_b, blocks_u, blocks_v)


    def to_owner(mine, away, zero, index):
        with jax.named_scope(f"P_F{index}"):
            came = [lax.ppermute(part, AXES, turn) for part, turn in zip(away, first_turn)]
        mine, *away = [mine[k] + came[0][k] + came[1][k] + came[2][k] for k in range(4)]
        with jax.named_scope(f"P_G{index}"):
            came = [lax.ppermute(part, AXES, turn) for part, turn in zip(away, second_turn)]
        return mine + (came[0] + zero) + came[1] + came[2]

    mine, *away, done_0 = apply_blocks(table, held_0, blocks, 0)
    *parts_1, done_0 = lax.optimization_barrier((own_1, left_1, across_1, right_1, done_0))
    results = [to_owner(mine, away, done_0[0, 0], 0)]
    mine, *away, done_1 = apply_blocks(table, both_cores(parts_1, 1), blocks, 1)
    results.append(to_owner(mine, away, done_1[0, 0], 1))
    parts = [r[:, :HALF] for r in results] + [r[:, HALF:] for r in results]
    return jnp.concatenate(parts, axis=1)


def solution(mesh):
    finer = Mesh(mesh.devices.reshape(SIZES), AXES)
    blocks = P(None, AXES, None, None)
    in_specs = (
        P("dir", None),
        P(None, ("y", "zhi", "x", "core"), "dir"),
        blocks,
        P(AXES, None),
        blocks,
        blocks,
        P(AXES, None),
        P(AXES),
        P(AXES, None),
    )
    out_specs = P(("x", "core", "dir", "y", "zhi"), None)
    return jax.shard_map(shards, mesh=finer, in_specs=in_specs, out_specs=out_specs, check_vma=False)
```

```python
import functools

import jax
import jax.numpy as jnp
from jax import lax
from jax.experimental import pallas as pl
from jax.experimental.pallas import tpu as pltpu
from jax.sharding import Mesh
from jax.sharding import PartitionSpec as P

AXES = ("dir", "y", "zhi", "x", "core")
ROW = ("y", "zhi")
COL = ("x", "core")
SIZES = (2, 4, 2, 4, 2)
CHUNKS = 2
COST = (40 << 30, 40 << 30)
CLUSTER = 512
HALF = 128
WIDE = 2 * HALF
PAD = 128
NEAR = 8
FAR = 4
VMEM_LIMIT = 60 << 20
SCOPED = 10 << 20

ANY = pl.BlockSpec(memory_space=pl.ANY)
SMEM = pl.BlockSpec(memory_space=pltpu.SMEM)
VMEM = pl.BlockSpec(memory_space=pltpu.VMEM)
HBM = pl.BlockSpec(memory_space=pltpu.HBM)
TOKEN = jax.ShapeDtypeStruct((8, 128), jnp.float32)

N_NEAR, N_FAR, NEAR_A, NEAR_B, FAR_A, FAR_B, RANK, ORDER, CORE, X = 0, 1, 2, 10, 18, 22, 26, 30, 46, 47


def split(values):
    high = values.astype(jnp.bfloat16)
    low = (values - high.astype(jnp.float32)).astype(jnp.bfloat16)
    return high, low


def dot(left, right):
    return jnp.dot(left, right, preferred_element_type=jnp.float32)


def rotations():
    tables = []
    for first in (True, False):
        for shift in (1, 2, 3):
            pairs = []
            for lo in range(2):
                for y in range(4):
                    for hi in range(2):
                        for x in range(4):
                            for core in range(2):
                                z = hi * 2 + lo
                                if (core == 0) == first:
                                    to_y, to_z = (y + shift) % 4, z
                                else:
                                    to_y, to_z = y, (z + shift) % 4
                                here = (((lo * 4 + y) * 2 + hi) * 4 + x) * 2 + core
                                there = (((to_z % 2 * 4 + to_y) * 2 + to_z // 2) * 4 + x) * 2 + core
                                pairs.append((here, there))
            tables.append(pairs)
    return tables[:3], tables[3:]


def rhs_kernel(cot_ref, rad_ref, out_0, out_1, cot, rad, sem_c, sem_r):
    width = cot.shape[1] // 2
    rows = rad.shape[1] // sem_r.shape[0]
    copies = [pltpu.make_async_copy(cot_ref, cot, sem_c.at[0])]
    for i in range(sem_r.shape[0]):
        tile = pl.ds(i * rows, rows)
        copies.append(pltpu.make_async_copy(rad_ref.at[:, tile], rad.at[:, tile], sem_r.at[i]))
    for copy in copies:
        copy.start()
    copies[0].wait()
    for i, copy in enumerate(copies[1:]):
        tile = slice(i * rows, (i + 1) * rows)
        copy.wait()
        for chunk, out_ref in enumerate((out_0, out_1)):
            re = cot[:, chunk * HALF : (chunk + 1) * HALF]
            im = cot[:, width + chunk * HALF : width + (chunk + 1) * HALF]
            out_ref[tile] = dot(rad[0, tile], jnp.concatenate([re, im], 1)) + dot(
                rad[1, tile], jnp.concatenate([-im, re], 1)
            )


def partial_rhs(cotangent, radiation):
    rows = radiation.shape[1]
    return pl.pallas_call(
        rhs_kernel,
        name="rhs",
        in_specs=[HBM, HBM],
        out_specs=[VMEM] * CHUNKS,
        out_shape=[pltpu.VMEM((rows, WIDE), jnp.float32)] * CHUNKS,
        scratch_shapes=[
            pltpu.VMEM(cotangent.shape, cotangent.dtype),
            pltpu.VMEM(radiation.shape, radiation.dtype),
            pltpu.SemaphoreType.DMA((1,)),
            pltpu.SemaphoreType.DMA((2,)),
        ],
        compiler_params=pltpu.CompilerParams(vmem_limit_bytes=SCOPED),
        cost_estimate=pl.CostEstimate(flops=1 << 30, bytes_accessed=4 << 20, transcendentals=0),
    )(*(pltpu.with_memory_space_constraint(f, pltpu.HBM) for f in (cotangent, radiation)))


def prepare_near_kernel(first, table, z_ref, out_ref, token, z_in, sem_in):
    slots, buffers = out_ref.shape[0], z_in.shape[0]
    token[...] = jnp.zeros_like(token)
    live = jnp.clip(table[N_NEAR] - first, 0, slots)

    def fetch(s):
        b = lax.rem(s, buffers)
        return pltpu.make_async_copy(z_ref.at[:, first + s], z_in.at[b], sem_in.at[b])

    for ahead in range(buffers - 1):

        @pl.when(ahead < live)
        def _():
            fetch(ahead).start()

    def near_step(s, _):
        @pl.when(s + buffers - 1 < live)
        def _():
            fetch(s + buffers - 1).start()

        fetch(s).wait()
        for part in range(2):
            high, low = split(z_in[lax.rem(s, buffers), part].T)
            out_ref[s, :, part * CLUSTER : (part + 1) * CLUSTER] = high
            out_ref[s, :, (part + 2) * CLUSTER : (part + 3) * CLUSTER] = low
        return 0

    lax.fori_loop(0, live, near_step, 0)


def prepare_near(table, near_z, first, slots):
    buffers = 3
    return pl.pallas_call(
        functools.partial(prepare_near_kernel, first),
        name=f"prepare_near_{first}",
        in_specs=[SMEM, HBM],
        out_specs=[VMEM, VMEM],
        out_shape=[pltpu.VMEM((slots, CLUSTER, 4 * CLUSTER), jnp.bfloat16), TOKEN],
        scratch_shapes=[
            pltpu.VMEM((buffers, 2, CLUSTER, CLUSTER), jnp.float32),
            pltpu.SemaphoreType.DMA((buffers,)),
        ],
        compiler_params=pltpu.CompilerParams(vmem_limit_bytes=SCOPED),
        cost_estimate=pl.CostEstimate(flops=1 << 28, bytes_accessed=slots << 21, transcendentals=0),
    )(table, pltpu.with_memory_space_constraint(near_z, pltpu.HBM))


def prepare_far_kernel(table, u_ref, v_ref, u_out, v_out, token, u_in, v_in, sem_u, sem_v):
    token[...] = jnp.zeros_like(token)
    far, rank_most = table[N_FAR], u_in.shape[2]

    def fetch(s):
        return (
            pltpu.make_async_copy(u_ref.at[:, s], u_in.at[s], sem_u.at[s]),
            pltpu.make_async_copy(v_ref.at[:, s], v_in.at[s], sem_v.at[s]),
        )

    def start(s, _):
        for copy in fetch(s):
            copy.start()
        return 0

    lax.fori_loop(0, far, start, 0)

    def far_step(s, _):
        for copy in fetch(s):
            copy.wait()
        live = lax.broadcasted_iota(jnp.int32, (PAD, CLUSTER), 0) < table[RANK + s]
        fill = jnp.zeros((PAD - rank_most, CLUSTER), jnp.float32)
        for part in range(2):
            padded = jnp.concatenate([u_in[s, part], fill], 0)
            high, low = split(jnp.where(live, padded, 0.0))
            u_out[s, :, part * CLUSTER : (part + 1) * CLUSTER] = high
            u_out[s, :, (part + 2) * CLUSTER : (part + 3) * CLUSTER] = low
            padded = jnp.concatenate([v_in[s, part], fill], 0)
            high, low = split(padded.T)
            v_out[s, :, part * PAD : (part + 1) * PAD] = high
            v_out[s, :, (part + 2) * PAD : (part + 3) * PAD] = low
        return 0

    lax.fori_loop(0, far, far_step, 0)


def prepare_far(table, far_ut, far_vt):
    rank_most = far_ut.shape[2]
    return pl.pallas_call(
        prepare_far_kernel,
        name="prepare_far",
        in_specs=[SMEM, HBM, HBM],
        out_specs=[VMEM, VMEM, VMEM],
        out_shape=[
            pltpu.VMEM((FAR, PAD, 4 * CLUSTER), jnp.bfloat16),
            pltpu.VMEM((FAR, CLUSTER, 4 * PAD), jnp.bfloat16),
            TOKEN,
        ],
        scratch_shapes=[
            pltpu.VMEM((FAR, 2, rank_most, CLUSTER), jnp.float32),
            pltpu.VMEM((FAR, 2, rank_most, CLUSTER), jnp.float32),
            pltpu.SemaphoreType.DMA((FAR,)),
            pltpu.SemaphoreType.DMA((FAR,)),
        ],
        compiler_params=pltpu.CompilerParams(vmem_limit_bytes=SCOPED),
        cost_estimate=pl.CostEstimate(flops=1 << 28, bytes_accessed=4 << 20, transcendentals=0),
    )(table, *(pltpu.with_memory_space_constraint(f, pltpu.HBM) for f in (far_ut, far_vt)))


def parts_of(values):
    high, low = split(values)
    high = jnp.concatenate([high, jnp.concatenate([-high[:, HALF:], high[:, :HALF]], 1)], 0)
    low = jnp.concatenate([low, jnp.concatenate([-low[:, HALF:], low[:, :HALF]], 1)], 0)
    return high, low


def product(left, values):
    high, low = parts_of(values)
    return dot(left, jnp.concatenate([high, high], 0)) + dot(left[:, : left.shape[1] // 2], low)


def pack_kernel(*refs):
    parts, out_ref, sem = refs[:-2], refs[-2], refs[-1]
    copies, first = [], 0
    for i, part in enumerate(parts):
        rows = part.shape[0]
        copies.append(pltpu.make_async_copy(part, out_ref.at[pl.ds(first, rows)], sem.at[i]))
        first += rows
    for copy in copies:
        copy.start()
    for copy in copies:
        copy.wait()


def pack(parts, index):
    rows = sum(part.shape[0] for part in parts)
    return pl.pallas_call(
        pack_kernel,
        name=f"pack_{index}",
        in_specs=[ANY] * len(parts),
        out_specs=ANY,
        out_shape=jax.ShapeDtypeStruct((rows, parts[0].shape[1]), jnp.float32),
        scratch_shapes=[pltpu.SemaphoreType.DMA((len(parts),))],
        compiler_params=pltpu.CompilerParams(vmem_limit_bytes=SCOPED),
        cost_estimate=pl.CostEstimate(flops=0, bytes_accessed=4 << 20, transcendentals=0),
    )(*parts)


def apply_kernel(table, *refs):
    held, (za_ref, zb_ref, u_ref, v_ref) = refs[:2], refs[2:6]
    outs, (token, x_buf, fx_buf, sem_x, sem_fx) = refs[6:11], refs[11:]
    turns = ((0, outs[0], 0, 4), (1, outs[1], 0, 4), (2, outs[2], 0, 2), (2, outs[3], 2, 4), (3, outs[4], 0, 4))
    near, far = table[N_NEAR], table[N_FAR]
    slots = za_ref.shape[0]

    def fetch(cluster, buf, sem):
        steps = lax.rem(table[X] + 4 - cluster // 2, 4)
        rows = pl.ds(pl.multiple_of(steps * CLUSTER, CLUSTER), CLUSTER)
        own_core = lax.rem(cluster, 2) == table[CORE]
        for ref, here in zip(held, (own_core, jnp.logical_not(own_core))):

            @pl.when(here)
            def _():
                pltpu.make_async_copy(ref.at[rows], buf, sem).start()

    def fetched(buf, sem):
        pltpu.make_async_copy(held[0].at[pl.ds(0, CLUSTER)], buf, sem).wait()

    def add(cluster, term):
        for half in range(2):
            rows = CLUSTER // 2
            place = table[ORDER + cluster * 2 + half]
            second = lax.rem(place, 4)
            for steps, out_ref, low, high in turns:

                @pl.when((place // 4 == steps) & (second >= low) & (second < high))
                def _():
                    out_ref[second - low] += term[half * rows : (half + 1) * rows]

    fetch(table[NEAR_A], x_buf.at[0], sem_x.at[0])

    def far_start(s, _):
        fetch(table[FAR_A + s], fx_buf.at[s], sem_fx.at[s])
        return 0

    lax.fori_loop(0, far, far_start, 0)
    for out_ref in (*outs, token):
        out_ref[...] = jnp.zeros_like(out_ref)

    def near_steps(z_ref, first, last):
        def near_step(s, _):
            b = lax.rem(s, 2)

            @pl.when(s + 1 < near)
            def _():
                fetch(table[NEAR_A + s + 1], x_buf.at[1 - b], sem_x.at[1 - b])

            fetched(x_buf.at[b], sem_x.at[b])
            add(table[NEAR_B + s], product(z_ref[s - first], x_buf[b]))
            return 0

        lax.fori_loop(first, last, near_step, 0)

    near_steps(za_ref, 0, jnp.minimum(near, slots))
    near_steps(zb_ref, slots, near)

    def far_step(s, _):
        fetched(fx_buf.at[s], sem_fx.at[s])
        add(table[FAR_B + s], product(v_ref[s], product(u_ref[s], fx_buf[s])))
        return 0

    lax.fori_loop(0, far, far_step, 0)


def apply_blocks(table, held, blocks, index):
    return pl.pallas_call(
        apply_kernel,
        name=f"apply_{index}",
        in_specs=[SMEM] + [ANY] * 2 + [VMEM] * 4,
        out_specs=[VMEM] * 6,
        out_shape=[jax.ShapeDtypeStruct((n, CLUSTER // 2, WIDE), jnp.float32) for n in (4, 4, 2, 2, 4)] + [TOKEN],
        scratch_shapes=[
            pltpu.VMEM((2, CLUSTER, WIDE), jnp.float32),
            pltpu.VMEM((FAR, CLUSTER, WIDE), jnp.float32),
            pltpu.SemaphoreType.DMA((2,)),
            pltpu.SemaphoreType.DMA((FAR,)),
        ],
        compiler_params=pltpu.CompilerParams(vmem_limit_bytes=SCOPED),
        cost_estimate=pl.CostEstimate(flops=COST[index], bytes_accessed=1, transcendentals=0),
    )(table, *held, *blocks)


def finish_kernel(*refs):
    parts, tokens, out_ref = refs[:8], refs[8:10], refs[10]
    for chunk in range(CHUNKS):
        own, *came = parts[chunk * 4 : chunk * 4 + 4]
        total = own[...] + came[0][...] + came[1][...] + came[2][...] + tokens[chunk][0, 0]
        for part in range(2):
            first = part * CHUNKS * HALF + chunk * HALF
            out_ref[:, first : first + HALF] = total[:, part * HALF : (part + 1) * HALF]


def finish(parts, tokens):
    rows = parts[0].shape[0]
    return pl.pallas_call(
        finish_kernel,
        name="finish",
        in_specs=[VMEM] * 10,
        out_specs=VMEM,
        out_shape=jax.ShapeDtypeStruct((rows, CHUNKS * WIDE), jnp.float32),
        compiler_params=pltpu.CompilerParams(vmem_limit_bytes=SCOPED),
        cost_estimate=pl.CostEstimate(flops=1 << 20, bytes_accessed=3 << 20, transcendentals=0),
    )(*parts, *tokens)


def scalars(near_pairs, far_pairs, far_ranks, block_counts):
    row_base = lax.axis_index(ROW) * 8
    col_base = lax.axis_index(COL) * 8
    core = lax.axis_index("core")
    index = lax.iota(jnp.int32, 16)
    steps_y = (index // 2 - lax.axis_index("y")) % 4
    steps_z = (index % 2 * 2 + index // 8 - lax.axis_index("zhi") * 2 - lax.axis_index("dir")) % 4
    order = jnp.where(core == 0, steps_y * 4 + steps_z, steps_z * 4 + steps_y)
    pieces = [
        block_counts[0],
        near_pairs[:, 0] - row_base,
        near_pairs[:, 1] - col_base,
        far_pairs[:, 0] - row_base,
        far_pairs[:, 1] - col_base,
        far_ranks,
        order,
        core[None],
        lax.axis_index("x")[None],
    ]
    return jnp.concatenate(pieces).astype(jnp.int32)


def shards(cotangent, radiation, near_z, near_pairs, far_ut, far_vt, far_pairs, far_ranks, block_counts):
    table = scalars(near_pairs, far_pairs, far_ranks, block_counts)
    own_0, own_1 = partial_rhs(cotangent, radiation)
    swap = [(0, 1), (1, 0)]
    first_turn, second_turn = rotations()

    def across_dir(part, name):
        with jax.named_scope(name):
            return lax.ppermute(part, "dir", swap)

    def step(part, k, name):
        with jax.named_scope(name):
            return lax.ppermute(part, "x", [(i, (i + k) % 4) for i in range(4)])

    def both_cores(parts, index):
        mine = pack(parts, index)
        with jax.named_scope(f"P_S{index}"):
            return mine, lax.ppermute(mine, "core", swap)

    middle = CLUSTER // 2
    blocks_a, done_a = prepare_near(table, near_z, 0, NEAR // 2)
    upper, lower = own_0[:middle], own_0[middle:]
    upper = upper + (across_dir(upper, "P_ZU") + done_a[0, 0])
    blocks_b, done_b = prepare_near(table, near_z, NEAR // 2, NEAR // 2)
    blocks_u, blocks_v, done_far = prepare_far(table, far_ut, far_vt)
    upper, lower = lax.optimization_barrier((upper, lower))
    left_u, right_u = step(upper, 1, "P_LU"), step(upper, 3, "P_RU")
    lower = lower + (across_dir(lower, "P_ZL") + done_b[0, 0])
    own_1, lower, left_u, right_u = lax.optimization_barrier((own_1, lower, left_u, right_u))
    left_l, right_l = step(lower, 1, "P_LL"), step(lower, 3, "P_RL")
    own_1 = own_1 + (across_dir(own_1, "P_Z1") + done_far[0, 0])
    upper_0, lower_0 = step(left_u, 1, "P_A0"), step(right_l, 3, "P_B0")
    own_1, upper_0, lower_0 = lax.optimization_barrier((own_1, upper_0, lower_0))
    left_1, right_1 = step(own_1, 1, "P_L1"), step(own_1, 3, "P_R1")
    across_1 = step(own_1, 2, "P_K1")
    held_0 = both_cores([upper, lower, left_u, left_l, upper_0, lower_0, right_u, right_l], 0)
    blocks = (blocks_a, blocks_b, blocks_u, blocks_v)


    def go(part, turn, name):
        with jax.named_scope(name):
            return lax.ppermute(part, AXES, turn)

    def first_step(upper, lower, index):
        return go(upper, first_turn[0], f"P_H{index}"), go(lower, first_turn[2], f"P_H{index}")

    def second_step(ahead, behind, came, index):
        ahead, behind = ahead.at[:2].add(came[0]), behind.at[2:].add(came[1])
        return go(ahead, first_turn[0], f"P_F{index}"), go(behind, first_turn[2], f"P_F{index}")

    def other_ring(mine, came, index):
        mine, *away = [mine[k] + came[0][k] + came[1][k] for k in range(4)]
        return mine, [go(part, turn, f"P_G{index}") for part, turn in zip(away, second_turn)]

    mine, ahead, upper_0, lower_0, behind, done_0 = apply_blocks(table, held_0, blocks, 0)
    came_0 = first_step(upper_0, lower_0, 0)
    *parts_1, came_u, came_l, done_0 = lax.optimization_barrier((own_1, left_1, across_1, right_1, *came_0, done_0))
    came_0 = came_u, came_l
    came_0 = second_step(ahead, behind, came_0, 0)
    mine_1, ahead, upper_1, lower_1, behind, done_1 = apply_blocks(table, both_cores(parts_1, 1), blocks, 1)
    upper_1, lower_1, *came_0 = lax.optimization_barrier((upper_1, lower_1, *came_0))
    first = other_ring(mine, came_0, 0)
    came_1 = second_step(ahead, behind, first_step(upper_1, lower_1, 1), 1)
    last = other_ring(mine_1, came_1, 1)
    return finish([first[0], *first[1], last[0], *last[1]], [done_0, done_1])


def solution(mesh):
    finer = Mesh(mesh.devices.reshape(SIZES), AXES)
    blocks = P(None, AXES, None, None)
    in_specs = (
        P("dir", None),
        P(None, ("y", "zhi", "x", "core"), "dir"),
        blocks,
        P(AXES, None),
        blocks,
        blocks,
        P(AXES, None),
        P(AXES),
        P(AXES, None),
    )
    out_specs = P(("x", "core", "dir", "y", "zhi"), None)
    return jax.shard_map(shards, mesh=finer, in_specs=in_specs, out_specs=out_specs, check_vma=False)
```

```python
import functools

import jax
import jax.numpy as jnp
from jax import lax
from jax.experimental import pallas as pl
from jax.experimental.pallas import tpu as pltpu
from jax.sharding import Mesh
from jax.sharding import PartitionSpec as P

AXES = ("dir", "y", "zhi", "x", "core")
ROW = ("y", "zhi")
COL = ("x", "core")
SIZES = (2, 4, 2, 4, 2)
CHUNKS = 2
COST = (40 << 30, 40 << 30)
CLUSTER = 512
HALF = 128
WIDE = 2 * HALF
PAD = 128
NEAR = 8
FAR = 4
VMEM_LIMIT = 60 << 20
SCOPED = 10 << 20

ANY = pl.BlockSpec(memory_space=pl.ANY)
SMEM = pl.BlockSpec(memory_space=pltpu.SMEM)
VMEM = pl.BlockSpec(memory_space=pltpu.VMEM)
HBM = pl.BlockSpec(memory_space=pltpu.HBM)
TOKEN = jax.ShapeDtypeStruct((8, 128), jnp.float32)

N_NEAR, N_FAR, NEAR_A, NEAR_B, FAR_A, FAR_B, RANK, ORDER, CORE, X = 0, 1, 2, 10, 18, 22, 26, 30, 46, 47


def split(values):
    high = values.astype(jnp.bfloat16)
    low = (values - high.astype(jnp.float32)).astype(jnp.bfloat16)
    return high, low


def dot(left, right):
    return jnp.dot(left, right, preferred_element_type=jnp.float32)


def rotations():
    tables = []
    for first in (True, False):
        for shift in (1, 2, 3):
            pairs = []
            for lo in range(2):
                for y in range(4):
                    for hi in range(2):
                        for x in range(4):
                            for core in range(2):
                                z = hi * 2 + lo
                                if (core == 0) == first:
                                    to_y, to_z = (y + shift) % 4, z
                                else:
                                    to_y, to_z = y, (z + shift) % 4
                                here = (((lo * 4 + y) * 2 + hi) * 4 + x) * 2 + core
                                there = (((to_z % 2 * 4 + to_y) * 2 + to_z // 2) * 4 + x) * 2 + core
                                pairs.append((here, there))
            tables.append(pairs)
    return tables[:3], tables[3:]


def rhs_kernel(cot_ref, rad_ref, out_0, out_1, cot, rad, sem_c, sem_r):
    width = cot.shape[1] // 2
    rows = rad.shape[1] // sem_r.shape[0]
    copies = [pltpu.make_async_copy(cot_ref, cot, sem_c.at[0])]
    for i in range(sem_r.shape[0]):
        tile = pl.ds(i * rows, rows)
        copies.append(pltpu.make_async_copy(rad_ref.at[:, tile], rad.at[:, tile], sem_r.at[i]))
    for copy in copies:
        copy.start()
    copies[0].wait()
    for i, copy in enumerate(copies[1:]):
        tile = slice(i * rows, (i + 1) * rows)
        copy.wait()
        for chunk, out_ref in enumerate((out_0, out_1)):
            re = cot[:, chunk * HALF : (chunk + 1) * HALF]
            im = cot[:, width + chunk * HALF : width + (chunk + 1) * HALF]
            out_ref[tile] = dot(rad[0, tile], jnp.concatenate([re, im], 1)) + dot(
                rad[1, tile], jnp.concatenate([-im, re], 1)
            )


def partial_rhs(cotangent, radiation):
    rows = radiation.shape[1]
    return pl.pallas_call(
        rhs_kernel,
        name="rhs",
        in_specs=[HBM, HBM],
        out_specs=[VMEM] * CHUNKS,
        out_shape=[pltpu.VMEM((rows, WIDE), jnp.float32)] * CHUNKS,
        scratch_shapes=[
            pltpu.VMEM(cotangent.shape, cotangent.dtype),
            pltpu.VMEM(radiation.shape, radiation.dtype),
            pltpu.SemaphoreType.DMA((1,)),
            pltpu.SemaphoreType.DMA((2,)),
        ],
        compiler_params=pltpu.CompilerParams(vmem_limit_bytes=SCOPED),
        cost_estimate=pl.CostEstimate(flops=1 << 30, bytes_accessed=4 << 20, transcendentals=0),
    )(*(pltpu.with_memory_space_constraint(f, pltpu.HBM) for f in (cotangent, radiation)))


def prepare_near_kernel(first, table, z_ref, out_ref, token, z_in, sem_in):
    slots, buffers = out_ref.shape[0], z_in.shape[0]
    token[...] = jnp.zeros_like(token)
    live = jnp.clip(table[N_NEAR] - first, 0, slots)

    def fetch(s):
        b = lax.rem(s, buffers)
        return pltpu.make_async_copy(z_ref.at[:, first + s], z_in.at[b], sem_in.at[b])

    for ahead in range(buffers - 1):

        @pl.when(ahead < live)
        def _():
            fetch(ahead).start()

    def near_step(s, _):
        @pl.when(s + buffers - 1 < live)
        def _():
            fetch(s + buffers - 1).start()

        fetch(s).wait()
        for part in range(2):
            high, low = split(z_in[lax.rem(s, buffers), part].T)
            out_ref[s, :, part * CLUSTER : (part + 1) * CLUSTER] = high
            out_ref[s, :, (part + 2) * CLUSTER : (part + 3) * CLUSTER] = low
        return 0

    lax.fori_loop(0, live, near_step, 0)


def prepare_near(table, near_z, first, slots):
    buffers = 3
    return pl.pallas_call(
        functools.partial(prepare_near_kernel, first),
        name=f"prepare_near_{first}",
        in_specs=[SMEM, HBM],
        out_specs=[VMEM, VMEM],
        out_shape=[pltpu.VMEM((slots, CLUSTER, 4 * CLUSTER), jnp.bfloat16), TOKEN],
        scratch_shapes=[
            pltpu.VMEM((buffers, 2, CLUSTER, CLUSTER), jnp.float32),
            pltpu.SemaphoreType.DMA((buffers,)),
        ],
        compiler_params=pltpu.CompilerParams(vmem_limit_bytes=SCOPED),
        cost_estimate=pl.CostEstimate(flops=1 << 28, bytes_accessed=slots << 21, transcendentals=0),
    )(table, pltpu.with_memory_space_constraint(near_z, pltpu.HBM))


def prepare_far_kernel(table, u_ref, v_ref, u_out, v_out, token, u_in, v_in, sem_u, sem_v):
    token[...] = jnp.zeros_like(token)
    far, rank_most = table[N_FAR], u_in.shape[2]

    def fetch(s):
        return (
            pltpu.make_async_copy(u_ref.at[:, s], u_in.at[s], sem_u.at[s]),
            pltpu.make_async_copy(v_ref.at[:, s], v_in.at[s], sem_v.at[s]),
        )

    def start(s, _):
        for copy in fetch(s):
            copy.start()
        return 0

    lax.fori_loop(0, far, start, 0)

    def far_step(s, _):
        for copy in fetch(s):
            copy.wait()
        live = lax.broadcasted_iota(jnp.int32, (PAD, CLUSTER), 0) < table[RANK + s]
        fill = jnp.zeros((PAD - rank_most, CLUSTER), jnp.float32)
        for part in range(2):
            padded = jnp.concatenate([u_in[s, part], fill], 0)
            high, low = split(jnp.where(live, padded, 0.0))
            u_out[s, :, part * CLUSTER : (part + 1) * CLUSTER] = high
            u_out[s, :, (part + 2) * CLUSTER : (part + 3) * CLUSTER] = low
            padded = jnp.concatenate([v_in[s, part], fill], 0)
            high, low = split(padded.T)
            v_out[s, :, part * PAD : (part + 1) * PAD] = high
            v_out[s, :, (part + 2) * PAD : (part + 3) * PAD] = low
        return 0

    lax.fori_loop(0, far, far_step, 0)


def prepare_far(table, far_ut, far_vt):
    rank_most = far_ut.shape[2]
    return pl.pallas_call(
        prepare_far_kernel,
        name="prepare_far",
        in_specs=[SMEM, HBM, HBM],
        out_specs=[VMEM, VMEM, VMEM],
        out_shape=[
            pltpu.VMEM((FAR, PAD, 4 * CLUSTER), jnp.bfloat16),
            pltpu.VMEM((FAR, CLUSTER, 4 * PAD), jnp.bfloat16),
            TOKEN,
        ],
        scratch_shapes=[
            pltpu.VMEM((FAR, 2, rank_most, CLUSTER), jnp.float32),
            pltpu.VMEM((FAR, 2, rank_most, CLUSTER), jnp.float32),
            pltpu.SemaphoreType.DMA((FAR,)),
            pltpu.SemaphoreType.DMA((FAR,)),
        ],
        compiler_params=pltpu.CompilerParams(vmem_limit_bytes=SCOPED),
        cost_estimate=pl.CostEstimate(flops=1 << 28, bytes_accessed=4 << 20, transcendentals=0),
    )(table, *(pltpu.with_memory_space_constraint(f, pltpu.HBM) for f in (far_ut, far_vt)))


def parts_of(values):
    high, low = split(values)
    high = jnp.concatenate([high, jnp.concatenate([-high[:, HALF:], high[:, :HALF]], 1)], 0)
    low = jnp.concatenate([low, jnp.concatenate([-low[:, HALF:], low[:, :HALF]], 1)], 0)
    return high, low


def product(left, values):
    high, low = parts_of(values)
    return dot(left, jnp.concatenate([high, high], 0)) + dot(left[:, : left.shape[1] // 2], low)


def pack_kernel(*refs):
    parts, out_ref, sem = refs[:-2], refs[-2], refs[-1]
    copies, first = [], 0
    for i, part in enumerate(parts):
        rows = part.shape[0]
        copies.append(pltpu.make_async_copy(part, out_ref.at[pl.ds(first, rows)], sem.at[i]))
        first += rows
    for copy in copies:
        copy.start()
    for copy in copies:
        copy.wait()


def pack(parts, index):
    rows = sum(part.shape[0] for part in parts)
    return pl.pallas_call(
        pack_kernel,
        name=f"pack_{index}",
        in_specs=[ANY] * len(parts),
        out_specs=ANY,
        out_shape=jax.ShapeDtypeStruct((rows, parts[0].shape[1]), jnp.float32),
        scratch_shapes=[pltpu.SemaphoreType.DMA((len(parts),))],
        compiler_params=pltpu.CompilerParams(vmem_limit_bytes=SCOPED),
        cost_estimate=pl.CostEstimate(flops=0, bytes_accessed=4 << 20, transcendentals=0),
    )(*parts)


def apply_kernel(table, *refs):
    held, (za_ref, zb_ref, u_ref, v_ref) = refs[:2], refs[2:6]
    outs, (token, x_buf, fx_buf, sem_x, sem_fx) = refs[6:11], refs[11:]
    turns = ((0, outs[0], 0, 4), (1, outs[1], 0, 4), (2, outs[2], 0, 2), (2, outs[3], 2, 4), (3, outs[4], 0, 4))
    near, far = table[N_NEAR], table[N_FAR]
    slots = za_ref.shape[0]

    def fetch(cluster, buf, sem):
        steps = lax.rem(table[X] + 4 - cluster // 2, 4)
        rows = pl.ds(pl.multiple_of(steps * CLUSTER, CLUSTER), CLUSTER)
        own_core = lax.rem(cluster, 2) == table[CORE]
        for ref, here in zip(held, (own_core, jnp.logical_not(own_core))):

            @pl.when(here)
            def _():
                pltpu.make_async_copy(ref.at[rows], buf, sem).start()

    def fetched(buf, sem):
        pltpu.make_async_copy(held[0].at[pl.ds(0, CLUSTER)], buf, sem).wait()

    def add(cluster, term):
        for half in range(2):
            rows = CLUSTER // 2
            place = table[ORDER + cluster * 2 + half]
            second = lax.rem(place, 4)
            for steps, out_ref, low, high in turns:

                @pl.when((place // 4 == steps) & (second >= low) & (second < high))
                def _():
                    out_ref[second - low] += term[half * rows : (half + 1) * rows]

    def fetch_near(s):
        @pl.when(s < near)
        def _():
            b = lax.rem(s, 4)
            fetch(table[NEAR_A + jnp.minimum(s, NEAR - 1)], x_buf.at[b], sem_x.at[b])

    def near_term(z_ref, first, s):
        b = lax.rem(s, 4)
        return product(z_ref[s - first], x_buf[b])

    def near_ready(s):
        b = lax.rem(s, 4)
        fetched(x_buf.at[b], sem_x.at[b])

    def far_term(s):
        return product(v_ref[s], product(u_ref[s], fx_buf[s]))

    fetch_near(0)
    fetch_near(1)

    def far_start(s, _):
        fetch(table[FAR_A + s], fx_buf.at[s], sem_fx.at[s])
        return 0

    lax.fori_loop(0, far, far_start, 0)
    for out_ref in (*outs, token):
        out_ref[...] = jnp.zeros_like(out_ref)

    def both_step(s, _):
        fetch_near(s + 2)
        near_ready(s)
        fetched(fx_buf.at[s], sem_fx.at[s])
        near_part, far_part = near_term(za_ref, 0, s), far_term(s)
        add(table[NEAR_B + s], near_part)
        add(table[FAR_B + s], far_part)
        return 0

    def near_step(z_ref, first):
        def step(s, _):
            fetch_near(s + 2)
            near_ready(s)
            add(table[NEAR_B + s], near_term(z_ref, first, s))
            return 0

        return step

    def near_steps(z_ref, first, start, stop):
        pairs = lax.div(stop - start, 2)

        def two_steps(i, _):
            s = start + 2 * i
            fetch_near(s + 2)
            fetch_near(s + 3)
            near_ready(s)
            near_ready(s + 1)
            terms = near_term(z_ref, first, s), near_term(z_ref, first, s + 1)
            add(table[NEAR_B + s], terms[0])
            add(table[NEAR_B + s + 1], terms[1])
            return 0

        lax.fori_loop(0, pairs, two_steps, 0)
        lax.fori_loop(start + 2 * pairs, stop, near_step(z_ref, first), 0)

    together = jnp.minimum(near, far)
    lax.fori_loop(0, together, both_step, 0)
    first_stop = jnp.minimum(near, slots)
    near_steps(za_ref, 0, together, first_stop)
    near_steps(zb_ref, slots, first_stop, near)

    def far_step(s, _):
        fetched(fx_buf.at[s], sem_fx.at[s])
        add(table[FAR_B + s], far_term(s))
        return 0

    lax.fori_loop(together, far, far_step, 0)


def apply_blocks(table, held, blocks, index):
    return pl.pallas_call(
        apply_kernel,
        name=f"apply_{index}",
        in_specs=[SMEM] + [ANY] * 2 + [VMEM] * 4,
        out_specs=[VMEM] * 6,
        out_shape=[jax.ShapeDtypeStruct((n, CLUSTER // 2, WIDE), jnp.float32) for n in (4, 4, 2, 2, 4)] + [TOKEN],
        scratch_shapes=[
            pltpu.VMEM((4, CLUSTER, WIDE), jnp.float32),
            pltpu.VMEM((FAR, CLUSTER, WIDE), jnp.float32),
            pltpu.SemaphoreType.DMA((4,)),
            pltpu.SemaphoreType.DMA((FAR,)),
        ],
        compiler_params=pltpu.CompilerParams(vmem_limit_bytes=SCOPED),
        cost_estimate=pl.CostEstimate(flops=COST[index], bytes_accessed=1, transcendentals=0),
    )(table, *held, *blocks)


def finish_kernel(*refs):
    parts, tokens, out_ref = refs[:8], refs[8:10], refs[10]
    for chunk in range(CHUNKS):
        own, *came = parts[chunk * 4 : chunk * 4 + 4]
        total = own[...] + came[0][...] + came[1][...] + came[2][...] + tokens[chunk][0, 0]
        for part in range(2):
            first = part * CHUNKS * HALF + chunk * HALF
            out_ref[:, first : first + HALF] = total[:, part * HALF : (part + 1) * HALF]


def finish(parts, tokens):
    rows = parts[0].shape[0]
    return pl.pallas_call(
        finish_kernel,
        name="finish",
        in_specs=[VMEM] * 10,
        out_specs=VMEM,
        out_shape=jax.ShapeDtypeStruct((rows, CHUNKS * WIDE), jnp.float32),
        compiler_params=pltpu.CompilerParams(vmem_limit_bytes=SCOPED),
        cost_estimate=pl.CostEstimate(flops=1 << 20, bytes_accessed=3 << 20, transcendentals=0),
    )(*parts, *tokens)


def scalars(near_pairs, far_pairs, far_ranks, block_counts):
    row_base = lax.axis_index(ROW) * 8
    col_base = lax.axis_index(COL) * 8
    core = lax.axis_index("core")
    index = lax.iota(jnp.int32, 16)
    steps_y = (index // 2 - lax.axis_index("y")) % 4
    steps_z = (index % 2 * 2 + index // 8 - lax.axis_index("zhi") * 2 - lax.axis_index("dir")) % 4
    order = jnp.where(core == 0, steps_y * 4 + steps_z, steps_z * 4 + steps_y)
    pieces = [
        block_counts[0],
        near_pairs[:, 0] - row_base,
        near_pairs[:, 1] - col_base,
        far_pairs[:, 0] - row_base,
        far_pairs[:, 1] - col_base,
        far_ranks,
        order,
        core[None],
        lax.axis_index("x")[None],
    ]
    return jnp.concatenate(pieces).astype(jnp.int32)


def shards(cotangent, radiation, near_z, near_pairs, far_ut, far_vt, far_pairs, far_ranks, block_counts):
    table = scalars(near_pairs, far_pairs, far_ranks, block_counts)
    own_0, own_1 = partial_rhs(cotangent, radiation)
    swap = [(0, 1), (1, 0)]
    first_turn, second_turn = rotations()

    def across_dir(part, name):
        with jax.named_scope(name):
            return lax.ppermute(part, "dir", swap)

    def step(part, k, name):
        with jax.named_scope(name):
            return lax.ppermute(part, "x", [(i, (i + k) % 4) for i in range(4)])

    def both_cores(parts, index):
        mine = pack(parts, index)
        with jax.named_scope(f"P_S{index}"):
            return mine, lax.ppermute(mine, "core", swap)

    middle = CLUSTER // 2
    blocks_a, done_a = prepare_near(table, near_z, 0, NEAR // 2)
    upper, lower = own_0[:middle], own_0[middle:]
    upper = upper + (across_dir(upper, "P_ZU") + done_a[0, 0])
    blocks_b, done_b = prepare_near(table, near_z, NEAR // 2, NEAR // 2)
    blocks_u, blocks_v, done_far = prepare_far(table, far_ut, far_vt)
    upper, lower = lax.optimization_barrier((upper, lower))
    left_u, right_u = step(upper, 1, "P_LU"), step(upper, 3, "P_RU")
    lower = lower + (across_dir(lower, "P_ZL") + done_b[0, 0])
    own_1, lower, left_u, right_u = lax.optimization_barrier((own_1, lower, left_u, right_u))
    left_l, right_l = step(lower, 1, "P_LL"), step(lower, 3, "P_RL")
    own_1 = own_1 + (across_dir(own_1, "P_Z1") + done_far[0, 0])
    upper_0, lower_0 = step(left_u, 1, "P_A0"), step(right_l, 3, "P_B0")
    own_1, upper_0, lower_0 = lax.optimization_barrier((own_1, upper_0, lower_0))
    left_1, right_1 = step(own_1, 1, "P_L1"), step(own_1, 3, "P_R1")
    across_1 = step(own_1, 2, "P_K1")
    held_0 = both_cores([upper, lower, left_u, left_l, upper_0, lower_0, right_u, right_l], 0)
    blocks = (blocks_a, blocks_b, blocks_u, blocks_v)


    def go(part, turn, name):
        with jax.named_scope(name):
            return lax.ppermute(part, AXES, turn)

    def first_step(upper, lower, index):
        return go(upper, first_turn[0], f"P_H{index}"), go(lower, first_turn[2], f"P_H{index}")

    def second_step(ahead, behind, came, index):
        ahead, behind = ahead.at[:2].add(came[0]), behind.at[2:].add(came[1])
        return go(ahead, first_turn[0], f"P_F{index}"), go(behind, first_turn[2], f"P_F{index}")

    def other_ring(mine, came, index):
        mine, *away = [mine[k] + came[0][k] + came[1][k] for k in range(4)]
        return mine, [go(part, turn, f"P_G{index}") for part, turn in zip(away, second_turn)]

    mine, ahead, upper_0, lower_0, behind, done_0 = apply_blocks(table, held_0, blocks, 0)
    came_0 = first_step(upper_0, lower_0, 0)
    *parts_1, came_u, came_l, done_0 = lax.optimization_barrier((own_1, left_1, across_1, right_1, *came_0, done_0))
    came_0 = came_u, came_l
    came_0 = second_step(ahead, behind, came_0, 0)
    mine_1, ahead, upper_1, lower_1, behind, done_1 = apply_blocks(table, both_cores(parts_1, 1), blocks, 1)
    upper_1, lower_1, *came_0 = lax.optimization_barrier((upper_1, lower_1, *came_0))
    first = other_ring(mine, came_0, 0)
    came_1 = second_step(ahead, behind, first_step(upper_1, lower_1, 1), 1)
    last = other_ring(mine_1, came_1, 1)
    return finish([first[0], *first[1], last[0], *last[1]], [done_0, done_1])


def solution(mesh):
    finer = Mesh(mesh.devices.reshape(SIZES), AXES)
    blocks = P(None, AXES, None, None)
    in_specs = (
        P("dir", None),
        P(None, ("y", "zhi", "x", "core"), "dir"),
        blocks,
        P(AXES, None),
        blocks,
        blocks,
        P(AXES, None),
        P(AXES),
        P(AXES, None),
    )
    out_specs = P(("x", "core", "dir", "y", "zhi"), None)
    return jax.shard_map(shards, mesh=finer, in_specs=in_specs, out_specs=out_specs, check_vma=False)
```

```python
import functools

import jax
import jax.numpy as jnp
from jax import lax
from jax.experimental import pallas as pl
from jax.experimental.pallas import tpu as pltpu
from jax.sharding import Mesh
from jax.sharding import PartitionSpec as P

AXES = ("dir", "y", "zhi", "x", "core")
ROW = ("y", "zhi")
COL = ("x", "core")
SIZES = (2, 4, 2, 4, 2)
CHUNKS = 2
COST = (40 << 30, 40 << 30)
CLUSTER = 512
HALF = 128
WIDE = 2 * HALF
PAD = 128
NEAR = 8
FAR = 4
VMEM_LIMIT = 60 << 20
SCOPED = 10 << 20

ANY = pl.BlockSpec(memory_space=pl.ANY)
SMEM = pl.BlockSpec(memory_space=pltpu.SMEM)
VMEM = pl.BlockSpec(memory_space=pltpu.VMEM)
HBM = pl.BlockSpec(memory_space=pltpu.HBM)
TOKEN = jax.ShapeDtypeStruct((8, 128), jnp.float32)

N_NEAR, N_FAR, NEAR_A, NEAR_B, FAR_A, FAR_B, RANK, ORDER, CORE, X = 0, 1, 2, 10, 18, 22, 26, 30, 46, 47


def split(values):
    high = values.astype(jnp.bfloat16)
    low = (values - high.astype(jnp.float32)).astype(jnp.bfloat16)
    return high, low


def dot(left, right):
    return jnp.dot(left, right, preferred_element_type=jnp.float32)


def rotations():
    tables = []
    for first in (True, False):
        for shift in (1, 2, 3):
            pairs = []
            for lo in range(2):
                for y in range(4):
                    for hi in range(2):
                        for x in range(4):
                            for core in range(2):
                                z = hi * 2 + lo
                                if (core == 0) == first:
                                    to_y, to_z = (y + shift) % 4, z
                                else:
                                    to_y, to_z = y, (z + shift) % 4
                                here = (((lo * 4 + y) * 2 + hi) * 4 + x) * 2 + core
                                there = (((to_z % 2 * 4 + to_y) * 2 + to_z // 2) * 4 + x) * 2 + core
                                pairs.append((here, there))
            tables.append(pairs)
    return tables[:3], tables[3:]


def rhs_kernel(cot_ref, rad_ref, out_0, out_1, cot, rad, sem_c, sem_r):
    width = cot.shape[1] // 2
    rows = rad.shape[1] // sem_r.shape[0]
    copies = [pltpu.make_async_copy(cot_ref, cot, sem_c.at[0])]
    for i in range(sem_r.shape[0]):
        tile = pl.ds(i * rows, rows)
        copies.append(pltpu.make_async_copy(rad_ref.at[:, tile], rad.at[:, tile], sem_r.at[i]))
    for copy in copies:
        copy.start()
    copies[0].wait()
    for i, copy in enumerate(copies[1:]):
        tile = slice(i * rows, (i + 1) * rows)
        copy.wait()
        for chunk, out_ref in enumerate((out_0, out_1)):
            re = cot[:, chunk * HALF : (chunk + 1) * HALF]
            im = cot[:, width + chunk * HALF : width + (chunk + 1) * HALF]
            out_ref[tile] = dot(rad[0, tile], jnp.concatenate([re, im], 1)) + dot(
                rad[1, tile], jnp.concatenate([-im, re], 1)
            )


def partial_rhs(cotangent, radiation):
    rows = radiation.shape[1]
    return pl.pallas_call(
        rhs_kernel,
        name="rhs",
        in_specs=[HBM, HBM],
        out_specs=[VMEM] * CHUNKS,
        out_shape=[pltpu.VMEM((rows, WIDE), jnp.float32)] * CHUNKS,
        scratch_shapes=[
            pltpu.VMEM(cotangent.shape, cotangent.dtype),
            pltpu.VMEM(radiation.shape, radiation.dtype),
            pltpu.SemaphoreType.DMA((1,)),
            pltpu.SemaphoreType.DMA((2,)),
        ],
        compiler_params=pltpu.CompilerParams(vmem_limit_bytes=SCOPED),
        cost_estimate=pl.CostEstimate(flops=1 << 30, bytes_accessed=4 << 20, transcendentals=0),
    )(*(pltpu.with_memory_space_constraint(f, pltpu.HBM) for f in (cotangent, radiation)))


def prepare_near_kernel(first, table, z_ref, out_ref, token, z_in, sem_in):
    slots, buffers = out_ref.shape[0], z_in.shape[0]
    token[...] = jnp.zeros_like(token)
    live = jnp.clip(table[N_NEAR] - first, 0, slots)

    def fetch(s):
        b = lax.rem(s, buffers)
        return pltpu.make_async_copy(z_ref.at[:, first + s], z_in.at[b], sem_in.at[b])

    for ahead in range(buffers - 1):

        @pl.when(ahead < live)
        def _():
            fetch(ahead).start()

    def near_step(s, _):
        @pl.when(s + buffers - 1 < live)
        def _():
            fetch(s + buffers - 1).start()

        fetch(s).wait()
        for part in range(2):
            high, low = split(z_in[lax.rem(s, buffers), part].T)
            out_ref[s, :, part * CLUSTER : (part + 1) * CLUSTER] = high
            out_ref[s, :, (part + 2) * CLUSTER : (part + 3) * CLUSTER] = low
        return 0

    lax.fori_loop(0, live, near_step, 0)


def prepare_near(table, near_z, first, slots):
    buffers = 3
    return pl.pallas_call(
        functools.partial(prepare_near_kernel, first),
        name=f"prepare_near_{first}",
        in_specs=[SMEM, HBM],
        out_specs=[VMEM, VMEM],
        out_shape=[pltpu.VMEM((slots, CLUSTER, 4 * CLUSTER), jnp.bfloat16), TOKEN],
        scratch_shapes=[
            pltpu.VMEM((buffers, 2, CLUSTER, CLUSTER), jnp.float32),
            pltpu.SemaphoreType.DMA((buffers,)),
        ],
        compiler_params=pltpu.CompilerParams(vmem_limit_bytes=SCOPED),
        cost_estimate=pl.CostEstimate(flops=1 << 28, bytes_accessed=slots << 21, transcendentals=0),
    )(table, pltpu.with_memory_space_constraint(near_z, pltpu.HBM))


def prepare_far_kernel(table, u_ref, v_ref, u_out, v_out, token, u_in, v_in, sem_u, sem_v):
    token[...] = jnp.zeros_like(token)
    far, rank_most = table[N_FAR], u_in.shape[2]

    def fetch(s):
        return (
            pltpu.make_async_copy(u_ref.at[:, s], u_in.at[s], sem_u.at[s]),
            pltpu.make_async_copy(v_ref.at[:, s], v_in.at[s], sem_v.at[s]),
        )

    def start(s, _):
        for copy in fetch(s):
            copy.start()
        return 0

    lax.fori_loop(0, far, start, 0)

    def far_step(s, _):
        for copy in fetch(s):
            copy.wait()
        live = lax.broadcasted_iota(jnp.int32, (PAD, CLUSTER), 0) < table[RANK + s]
        fill = jnp.zeros((PAD - rank_most, CLUSTER), jnp.float32)
        for part in range(2):
            padded = jnp.concatenate([u_in[s, part], fill], 0)
            high, low = split(jnp.where(live, padded, 0.0))
            u_out[s, :, part * CLUSTER : (part + 1) * CLUSTER] = high
            u_out[s, :, (part + 2) * CLUSTER : (part + 3) * CLUSTER] = low
            padded = jnp.concatenate([v_in[s, part], fill], 0)
            high, low = split(padded.T)
            v_out[s, :, part * PAD : (part + 1) * PAD] = high
            v_out[s, :, (part + 2) * PAD : (part + 3) * PAD] = low
        return 0

    lax.fori_loop(0, far, far_step, 0)


def prepare_far(table, far_ut, far_vt):
    rank_most = far_ut.shape[2]
    return pl.pallas_call(
        prepare_far_kernel,
        name="prepare_far",
        in_specs=[SMEM, HBM, HBM],
        out_specs=[VMEM, VMEM, VMEM],
        out_shape=[
            pltpu.VMEM((FAR, PAD, 4 * CLUSTER), jnp.bfloat16),
            pltpu.VMEM((FAR, CLUSTER, 4 * PAD), jnp.bfloat16),
            TOKEN,
        ],
        scratch_shapes=[
            pltpu.VMEM((FAR, 2, rank_most, CLUSTER), jnp.float32),
            pltpu.VMEM((FAR, 2, rank_most, CLUSTER), jnp.float32),
            pltpu.SemaphoreType.DMA((FAR,)),
            pltpu.SemaphoreType.DMA((FAR,)),
        ],
        compiler_params=pltpu.CompilerParams(vmem_limit_bytes=SCOPED),
        cost_estimate=pl.CostEstimate(flops=1 << 28, bytes_accessed=4 << 20, transcendentals=0),
    )(table, *(pltpu.with_memory_space_constraint(f, pltpu.HBM) for f in (far_ut, far_vt)))


def parts_of(values):
    high, low = split(values)
    high = jnp.concatenate([high, jnp.concatenate([-high[:, HALF:], high[:, :HALF]], 1)], 0)
    low = jnp.concatenate([low, jnp.concatenate([-low[:, HALF:], low[:, :HALF]], 1)], 0)
    return high, low


def product(left, values):
    high, low = parts_of(values)
    return dot(left, jnp.concatenate([high, high], 0)) + dot(left[:, : left.shape[1] // 2], low)


def pack_kernel(*refs):
    parts, out_ref, sem = refs[:-2], refs[-2], refs[-1]
    copies, first = [], 0
    for i, part in enumerate(parts):
        rows = part.shape[0]
        copies.append(pltpu.make_async_copy(part, out_ref.at[pl.ds(first, rows)], sem.at[i]))
        first += rows
    for copy in copies:
        copy.start()
    for copy in copies:
        copy.wait()


def pack(parts, index):
    rows = sum(part.shape[0] for part in parts)
    return pl.pallas_call(
        pack_kernel,
        name=f"pack_{index}",
        in_specs=[ANY] * len(parts),
        out_specs=ANY,
        out_shape=jax.ShapeDtypeStruct((rows, parts[0].shape[1]), jnp.float32),
        scratch_shapes=[pltpu.SemaphoreType.DMA((len(parts),))],
        compiler_params=pltpu.CompilerParams(vmem_limit_bytes=SCOPED),
        cost_estimate=pl.CostEstimate(flops=0, bytes_accessed=4 << 20, transcendentals=0),
    )(*parts)


def apply_kernel(table, *refs):
    held, (za_ref, zb_ref, u_ref, v_ref) = refs[:2], refs[2:6]
    outs, (token, x_buf, fx_buf, sem_x, sem_fx) = refs[6:11], refs[11:]
    turns = ((0, outs[0], 0, 4), (1, outs[1], 0, 4), (2, outs[2], 0, 2), (2, outs[3], 2, 4), (3, outs[4], 0, 4))
    near, far = table[N_NEAR], table[N_FAR]
    slots = za_ref.shape[0]

    def fetch(cluster, buf, sem):
        steps = lax.rem(table[X] + 4 - cluster // 2, 4)
        rows = pl.ds(pl.multiple_of(steps * CLUSTER, CLUSTER), CLUSTER)
        own_core = lax.rem(cluster, 2) == table[CORE]
        for ref, here in zip(held, (own_core, jnp.logical_not(own_core))):

            @pl.when(here)
            def _():
                pltpu.make_async_copy(ref.at[rows], buf, sem).start()

    def fetched(buf, sem):
        pltpu.make_async_copy(held[0].at[pl.ds(0, CLUSTER)], buf, sem).wait()

    def add(cluster, term):
        for half in range(2):
            rows = CLUSTER // 2
            place = table[ORDER + cluster * 2 + half]
            second = lax.rem(place, 4)
            for steps, out_ref, low, high in turns:

                @pl.when((place // 4 == steps) & (second >= low) & (second < high))
                def _():
                    out_ref[second - low] += term[half * rows : (half + 1) * rows]

    def fetch_near(s):
        @pl.when(s < near)
        def _():
            b = lax.rem(s, 4)
            fetch(table[NEAR_A + jnp.minimum(s, NEAR - 1)], x_buf.at[b], sem_x.at[b])

    def near_term(z_ref, first, s):
        b = lax.rem(s, 4)
        return product(z_ref[s - first], x_buf[b])

    def near_ready(s):
        b = lax.rem(s, 4)
        fetched(x_buf.at[b], sem_x.at[b])

    def far_term(s):
        return product(v_ref[s], product(u_ref[s], fx_buf[s]))

    fetch_near(0)
    fetch_near(1)

    def far_start(s, _):
        fetch(table[FAR_A + s], fx_buf.at[s], sem_fx.at[s])
        return 0

    lax.fori_loop(0, far, far_start, 0)
    for out_ref in (*outs, token):
        out_ref[...] = jnp.zeros_like(out_ref)

    def both_step(s, _):
        fetch_near(s + 2)
        near_ready(s)
        fetched(fx_buf.at[s], sem_fx.at[s])
        near_part, far_part = near_term(za_ref, 0, s), far_term(s)
        add(table[NEAR_B + s], near_part)
        add(table[FAR_B + s], far_part)
        return 0

    def near_step(z_ref, first):
        def step(s, _):
            fetch_near(s + 2)
            near_ready(s)
            add(table[NEAR_B + s], near_term(z_ref, first, s))
            return 0

        return step

    def near_steps(z_ref, first, start, stop):
        pairs = lax.div(stop - start, 2)

        def two_steps(i, _):
            s = start + 2 * i
            fetch_near(s + 2)
            fetch_near(s + 3)
            near_ready(s)
            near_ready(s + 1)
            terms = near_term(z_ref, first, s), near_term(z_ref, first, s + 1)
            add(table[NEAR_B + s], terms[0])
            add(table[NEAR_B + s + 1], terms[1])
            return 0

        lax.fori_loop(0, pairs, two_steps, 0)
        lax.fori_loop(start + 2 * pairs, stop, near_step(z_ref, first), 0)

    together = jnp.minimum(near, far)
    lax.fori_loop(0, together, both_step, 0)
    first_stop = jnp.minimum(near, slots)
    near_steps(za_ref, 0, together, first_stop)
    near_steps(zb_ref, slots, first_stop, near)

    def far_step(s, _):
        fetched(fx_buf.at[s], sem_fx.at[s])
        add(table[FAR_B + s], far_term(s))
        return 0

    lax.fori_loop(together, far, far_step, 0)


def apply_blocks(table, held, blocks, index):
    return pl.pallas_call(
        apply_kernel,
        name=f"apply_{index}",
        in_specs=[SMEM] + [ANY] * 2 + [VMEM] * 4,
        out_specs=[VMEM] * 6,
        out_shape=[jax.ShapeDtypeStruct((n, CLUSTER // 2, WIDE), jnp.float32) for n in (4, 4, 2, 2, 4)] + [TOKEN],
        scratch_shapes=[
            pltpu.VMEM((4, CLUSTER, WIDE), jnp.float32),
            pltpu.VMEM((FAR, CLUSTER, WIDE), jnp.float32),
            pltpu.SemaphoreType.DMA((4,)),
            pltpu.SemaphoreType.DMA((FAR,)),
        ],
        compiler_params=pltpu.CompilerParams(vmem_limit_bytes=SCOPED),
        cost_estimate=pl.CostEstimate(flops=COST[index], bytes_accessed=1, transcendentals=0),
    )(table, *held, *blocks)


def finish_kernel(*refs):
    parts, tokens, out_ref = refs[:8], refs[8:10], refs[10]
    for chunk in range(CHUNKS):
        own, *came = parts[chunk * 4 : chunk * 4 + 4]
        total = own[...] + came[0][...] + came[1][...] + came[2][...] + tokens[chunk][0, 0]
        for part in range(2):
            first = part * CHUNKS * HALF + chunk * HALF
            out_ref[:, first : first + HALF] = total[:, part * HALF : (part + 1) * HALF]


def finish(parts, tokens):
    rows = parts[0].shape[0]
    return pl.pallas_call(
        finish_kernel,
        name="finish",
        in_specs=[VMEM] * 10,
        out_specs=VMEM,
        out_shape=jax.ShapeDtypeStruct((rows, CHUNKS * WIDE), jnp.float32),
        compiler_params=pltpu.CompilerParams(vmem_limit_bytes=SCOPED),
        cost_estimate=pl.CostEstimate(flops=1 << 20, bytes_accessed=3 << 20, transcendentals=0),
    )(*parts, *tokens)


def scalars(near_pairs, far_pairs, far_ranks, block_counts):
    row_base = lax.axis_index(ROW) * 8
    col_base = lax.axis_index(COL) * 8
    core = lax.axis_index("core")
    index = lax.iota(jnp.int32, 16)
    steps_y = (index // 2 - lax.axis_index("y")) % 4
    steps_z = (index % 2 * 2 + index // 8 - lax.axis_index("zhi") * 2 - lax.axis_index("dir")) % 4
    order = jnp.where(core == 0, steps_y * 4 + steps_z, steps_z * 4 + steps_y)
    pieces = [
        block_counts[0],
        near_pairs[:, 0] - row_base,
        near_pairs[:, 1] - col_base,
        far_pairs[:, 0] - row_base,
        far_pairs[:, 1] - col_base,
        far_ranks,
        order,
        core[None],
        lax.axis_index("x")[None],
    ]
    return jnp.concatenate(pieces).astype(jnp.int32)


def shards(cotangent, radiation, near_z, near_pairs, far_ut, far_vt, far_pairs, far_ranks, block_counts):
    table = scalars(near_pairs, far_pairs, far_ranks, block_counts)
    own_0, own_1 = partial_rhs(cotangent, radiation)
    swap = [(0, 1), (1, 0)]
    first_turn, second_turn = rotations()

    def across_dir(part, name):
        with jax.named_scope(name):
            return lax.ppermute(part, "dir", swap)

    def step(part, k, name):
        with jax.named_scope(name):
            return lax.ppermute(part, "x", [(i, (i + k) % 4) for i in range(4)])

    def both_cores(parts, index):
        mine = pack(parts, index)
        with jax.named_scope(f"P_S{index}"):
            return mine, lax.ppermute(mine, "core", swap)

    middle = CLUSTER // 2
    blocks_a, done_a = prepare_near(table, near_z, 0, NEAR // 2)
    upper, lower = own_0[:middle], own_0[middle:]
    upper = upper + (across_dir(upper, "P_ZU") + done_a[0, 0])
    blocks_b, done_b = prepare_near(table, near_z, NEAR // 2, NEAR // 2)
    upper, lower = lax.optimization_barrier((upper, lower))
    left_u, right_u = step(upper, 1, "P_LU"), step(upper, 3, "P_RU")
    lower = lower + (across_dir(lower, "P_ZL") + done_b[0, 0])
    own_1, lower, left_u, right_u = lax.optimization_barrier((own_1, lower, left_u, right_u))
    left_l, right_l = step(lower, 1, "P_LL"), step(lower, 3, "P_RL")
    came_1 = across_dir(own_1, "P_Z1")
    right_l, table_far = lax.optimization_barrier((right_l, table))
    blocks_u, blocks_v, done_far = prepare_far(table_far, far_ut, far_vt)
    upper_0, lower_0 = step(left_u, 1, "P_A0"), step(right_l, 3, "P_B0")
    own_1 = own_1 + (came_1 + done_far[0, 0])
    own_1, upper_0, lower_0 = lax.optimization_barrier((own_1, upper_0, lower_0))
    left_1, right_1 = step(own_1, 1, "P_L1"), step(own_1, 3, "P_R1")
    across_1 = step(own_1, 2, "P_K1")
    held_0 = both_cores([upper, lower, left_u, left_l, upper_0, lower_0, right_u, right_l], 0)
    blocks = (blocks_a, blocks_b, blocks_u, blocks_v)


    def go(part, turn, name):
        with jax.named_scope(name):
            return lax.ppermute(part, AXES, turn)

    def first_step(upper, lower, index):
        return go(upper, first_turn[0], f"P_H{index}"), go(lower, first_turn[2], f"P_H{index}")

    def second_step(ahead, behind, came, index):
        ahead, behind = ahead.at[:2].add(came[0]), behind.at[2:].add(came[1])
        return go(ahead, first_turn[0], f"P_F{index}"), go(behind, first_turn[2], f"P_F{index}")

    def other_ring(mine, came, index):
        mine, *away = [mine[k] + came[0][k] + came[1][k] for k in range(4)]
        return mine, [go(part, turn, f"P_G{index}") for part, turn in zip(away, second_turn)]

    mine, ahead, upper_0, lower_0, behind, done_0 = apply_blocks(table, held_0, blocks, 0)
    came_0 = first_step(upper_0, lower_0, 0)
    *parts_1, came_u, came_l, done_0 = lax.optimization_barrier((own_1, left_1, across_1, right_1, *came_0, done_0))
    came_0 = came_u, came_l
    came_0 = second_step(ahead, behind, came_0, 0)
    mine_1, ahead, upper_1, lower_1, behind, done_1 = apply_blocks(table, both_cores(parts_1, 1), blocks, 1)
    upper_1, lower_1, *came_0 = lax.optimization_barrier((upper_1, lower_1, *came_0))
    first = other_ring(mine, came_0, 0)
    came_1 = second_step(ahead, behind, first_step(upper_1, lower_1, 1), 1)
    last = other_ring(mine_1, came_1, 1)
    return finish([first[0], *first[1], last[0], *last[1]], [done_0, done_1])


def solution(mesh):
    finer = Mesh(mesh.devices.reshape(SIZES), AXES)
    blocks = P(None, AXES, None, None)
    in_specs = (
        P("dir", None),
        P(None, ("y", "zhi", "x", "core"), "dir"),
        blocks,
        P(AXES, None),
        blocks,
        blocks,
        P(AXES, None),
        P(AXES),
        P(AXES, None),
    )
    out_specs = P(("x", "core", "dir", "y", "zhi"), None)
    return jax.shard_map(shards, mesh=finer, in_specs=in_specs, out_specs=out_specs, check_vma=False)
```

```python
import functools

import jax
import jax.numpy as jnp
from jax import lax
from jax.experimental import pallas as pl
from jax.experimental.pallas import tpu as pltpu
from jax.sharding import Mesh
from jax.sharding import PartitionSpec as P

AXES = ("dir", "y", "zhi", "x", "core")
ROW = ("y", "zhi")
COL = ("x", "core")
SIZES = (2, 4, 2, 4, 2)
CHUNKS = 2
CLUSTER = 512
HALF = 128
WIDE = 2 * HALF
PAD = 128
NEAR = 8
FAR = 4
SCOPED = 10 << 20

ANY = pl.BlockSpec(memory_space=pl.ANY)
SMEM = pl.BlockSpec(memory_space=pltpu.SMEM)
VMEM = pl.BlockSpec(memory_space=pltpu.VMEM)
HBM = pl.BlockSpec(memory_space=pltpu.HBM)
TOKEN = jax.ShapeDtypeStruct((8, 128), jnp.float32)

N_NEAR, N_FAR, NEAR_A, NEAR_B, FAR_A, FAR_B, RANK, ORDER, CORE, X = 0, 1, 2, 10, 18, 22, 26, 30, 46, 47


def split(values):
    high = values.astype(jnp.bfloat16)
    low = (values - high.astype(jnp.float32)).astype(jnp.bfloat16)
    return high, low


def dot(left, right):
    return jnp.dot(left, right, preferred_element_type=jnp.float32)


def rotations():
    tables = []
    for first in (True, False):
        for shift in (1, 2, 3):
            pairs = []
            for lo in range(2):
                for y in range(4):
                    for hi in range(2):
                        for x in range(4):
                            for core in range(2):
                                z = hi * 2 + lo
                                if (core == 0) == first:
                                    to_y, to_z = (y + shift) % 4, z
                                else:
                                    to_y, to_z = y, (z + shift) % 4
                                here = (((lo * 4 + y) * 2 + hi) * 4 + x) * 2 + core
                                there = (((to_z % 2 * 4 + to_y) * 2 + to_z // 2) * 4 + x) * 2 + core
                                pairs.append((here, there))
            tables.append(pairs)
    return tables[:3], tables[3:]


def rhs_kernel(cot_ref, rad_ref, out_0, out_1, cot, rad, sem_c, sem_r):
    width = cot.shape[1] // 2
    rows = rad.shape[1] // sem_r.shape[0]
    copies = [pltpu.make_async_copy(cot_ref, cot, sem_c.at[0])]
    for i in range(sem_r.shape[0]):
        tile = pl.ds(i * rows, rows)
        copies.append(pltpu.make_async_copy(rad_ref.at[:, tile], rad.at[:, tile], sem_r.at[i]))
    for copy in copies:
        copy.start()
    copies[0].wait()
    for i, copy in enumerate(copies[1:]):
        tile = slice(i * rows, (i + 1) * rows)
        copy.wait()
        for chunk, out_ref in enumerate((out_0, out_1)):
            re = cot[:, chunk * HALF : (chunk + 1) * HALF]
            im = cot[:, width + chunk * HALF : width + (chunk + 1) * HALF]
            out_ref[tile] = dot(rad[0, tile], jnp.concatenate([re, im], 1)) + dot(
                rad[1, tile], jnp.concatenate([-im, re], 1)
            )


def partial_rhs(cotangent, radiation):
    rows = radiation.shape[1]
    return pl.pallas_call(
        rhs_kernel,
        name="rhs",
        in_specs=[HBM, HBM],
        out_specs=[VMEM] * CHUNKS,
        out_shape=[pltpu.VMEM((rows, WIDE), jnp.float32)] * CHUNKS,
        scratch_shapes=[
            pltpu.VMEM(cotangent.shape, cotangent.dtype),
            pltpu.VMEM(radiation.shape, radiation.dtype),
            pltpu.SemaphoreType.DMA((1,)),
            pltpu.SemaphoreType.DMA((2,)),
        ],
        compiler_params=pltpu.CompilerParams(vmem_limit_bytes=SCOPED),
        cost_estimate=pl.CostEstimate(flops=1 << 30, bytes_accessed=4 << 20, transcendentals=0),
    )(*(pltpu.with_memory_space_constraint(f, pltpu.HBM) for f in (cotangent, radiation)))


def prepare_near_kernel(first, table, z_ref, out_ref, token, z_in, sem_in):
    slots, buffers = out_ref.shape[0], z_in.shape[0]
    token[...] = jnp.zeros_like(token)
    live = jnp.clip(table[N_NEAR] - first, 0, slots)

    def fetch(s):
        b = lax.rem(s, buffers)
        return pltpu.make_async_copy(z_ref.at[:, first + s], z_in.at[b], sem_in.at[b])

    for ahead in range(buffers - 1):

        @pl.when(ahead < live)
        def _():
            fetch(ahead).start()

    def near_step(s, _):
        @pl.when(s + buffers - 1 < live)
        def _():
            fetch(s + buffers - 1).start()

        fetch(s).wait()
        for part in range(2):
            high, low = split(z_in[lax.rem(s, buffers), part].T)
            out_ref[s, :, part * CLUSTER : (part + 1) * CLUSTER] = high
            out_ref[s, :, (part + 2) * CLUSTER : (part + 3) * CLUSTER] = low
        return 0

    lax.fori_loop(0, live, near_step, 0)


def prepare_near(table, near_z, first, slots):
    buffers = 3
    return pl.pallas_call(
        functools.partial(prepare_near_kernel, first),
        name=f"prepare_near_{first}",
        in_specs=[SMEM, HBM],
        out_specs=[VMEM, VMEM],
        out_shape=[pltpu.VMEM((slots, CLUSTER, 4 * CLUSTER), jnp.bfloat16), TOKEN],
        scratch_shapes=[
            pltpu.VMEM((buffers, 2, CLUSTER, CLUSTER), jnp.float32),
            pltpu.SemaphoreType.DMA((buffers,)),
        ],
        compiler_params=pltpu.CompilerParams(vmem_limit_bytes=SCOPED),
        cost_estimate=pl.CostEstimate(flops=1 << 28, bytes_accessed=slots << 21, transcendentals=0),
    )(table, pltpu.with_memory_space_constraint(near_z, pltpu.HBM))


def prepare_far_kernel(table, u_ref, v_ref, u_out, v_out, token, u_in, v_in, sem_u, sem_v):
    token[...] = jnp.zeros_like(token)
    far, rank_most = table[N_FAR], u_in.shape[2]

    def fetch(s):
        return (
            pltpu.make_async_copy(u_ref.at[:, s], u_in.at[s], sem_u.at[s]),
            pltpu.make_async_copy(v_ref.at[:, s], v_in.at[s], sem_v.at[s]),
        )

    def start(s, _):
        for copy in fetch(s):
            copy.start()
        return 0

    lax.fori_loop(0, far, start, 0)

    def far_step(s, _):
        for copy in fetch(s):
            copy.wait()
        live = lax.broadcasted_iota(jnp.int32, (PAD, CLUSTER), 0) < table[RANK + s]
        fill = jnp.zeros((PAD - rank_most, CLUSTER), jnp.float32)
        for part in range(2):
            padded = jnp.concatenate([u_in[s, part], fill], 0)
            high, low = split(jnp.where(live, padded, 0.0))
            u_out[s, :, part * CLUSTER : (part + 1) * CLUSTER] = high
            u_out[s, :, (part + 2) * CLUSTER : (part + 3) * CLUSTER] = low
            padded = jnp.concatenate([v_in[s, part], fill], 0)
            high, low = split(padded.T)
            v_out[s, :, part * PAD : (part + 1) * PAD] = high
            v_out[s, :, (part + 2) * PAD : (part + 3) * PAD] = low
        return 0

    lax.fori_loop(0, far, far_step, 0)


def prepare_far(table, far_ut, far_vt):
    rank_most = far_ut.shape[2]
    return pl.pallas_call(
        prepare_far_kernel,
        name="prepare_far",
        in_specs=[SMEM, HBM, HBM],
        out_specs=[VMEM, VMEM, VMEM],
        out_shape=[
            pltpu.VMEM((FAR, PAD, 4 * CLUSTER), jnp.bfloat16),
            pltpu.VMEM((FAR, CLUSTER, 4 * PAD), jnp.bfloat16),
            TOKEN,
        ],
        scratch_shapes=[
            pltpu.VMEM((FAR, 2, rank_most, CLUSTER), jnp.float32),
            pltpu.VMEM((FAR, 2, rank_most, CLUSTER), jnp.float32),
            pltpu.SemaphoreType.DMA((FAR,)),
            pltpu.SemaphoreType.DMA((FAR,)),
        ],
        compiler_params=pltpu.CompilerParams(vmem_limit_bytes=SCOPED),
        cost_estimate=pl.CostEstimate(flops=1 << 28, bytes_accessed=4 << 20, transcendentals=0),
    )(table, *(pltpu.with_memory_space_constraint(f, pltpu.HBM) for f in (far_ut, far_vt)))


def parts_of(values):
    high, low = split(values)
    high = jnp.concatenate([high, jnp.concatenate([-high[:, HALF:], high[:, :HALF]], 1)], 0)
    low = jnp.concatenate([low, jnp.concatenate([-low[:, HALF:], low[:, :HALF]], 1)], 0)
    return high, low


def product(left, values):
    high, low = parts_of(values)
    return dot(left, jnp.concatenate([high, high], 0)) + dot(left[:, : left.shape[1] // 2], low)


def pack_kernel(*refs):
    parts, out_ref, sem = refs[:-2], refs[-2], refs[-1]
    copies, first = [], 0
    for i, part in enumerate(parts):
        rows = part.shape[0]
        copies.append(pltpu.make_async_copy(part, out_ref.at[pl.ds(first, rows)], sem.at[i]))
        first += rows
    for copy in copies:
        copy.start()
    for copy in copies:
        copy.wait()


def pack(parts, index):
    rows = sum(part.shape[0] for part in parts)
    return pl.pallas_call(
        pack_kernel,
        name=f"pack_{index}",
        in_specs=[ANY] * len(parts),
        out_specs=ANY,
        out_shape=jax.ShapeDtypeStruct((rows, parts[0].shape[1]), jnp.float32),
        scratch_shapes=[pltpu.SemaphoreType.DMA((len(parts),))],
        compiler_params=pltpu.CompilerParams(vmem_limit_bytes=SCOPED),
        cost_estimate=pl.CostEstimate(flops=0, bytes_accessed=4 << 20, transcendentals=0),
    )(*parts)


def apply_kernel(table, *refs):
    held, (za_ref, zb_ref, u_ref, v_ref) = refs[:2], refs[2:6]
    outs, (token, x_buf, fx_buf, sem_x, sem_fx) = refs[6:11], refs[11:]
    turns = ((0, outs[0], 0, 4), (1, outs[1], 0, 4), (2, outs[2], 0, 2), (2, outs[3], 2, 4), (3, outs[4], 0, 4))
    near, far = table[N_NEAR], table[N_FAR]
    slots = za_ref.shape[0]

    def fetch(cluster, buf, sem):
        steps = lax.rem(table[X] + 4 - cluster // 2, 4)
        rows = pl.ds(pl.multiple_of(steps * CLUSTER, CLUSTER), CLUSTER)
        own_core = lax.rem(cluster, 2) == table[CORE]
        for ref, here in zip(held, (own_core, jnp.logical_not(own_core))):

            @pl.when(here)
            def _():
                pltpu.make_async_copy(ref.at[rows], buf, sem).start()

    def fetched(buf, sem):
        pltpu.make_async_copy(held[0].at[pl.ds(0, CLUSTER)], buf, sem).wait()

    def add(cluster, term):
        for half in range(2):
            rows = CLUSTER // 2
            place = table[ORDER + cluster * 2 + half]
            second = lax.rem(place, 4)
            for steps, out_ref, low, high in turns:

                @pl.when((place // 4 == steps) & (second >= low) & (second < high))
                def _():
                    out_ref[second - low] += term[half * rows : (half + 1) * rows]

    def fetch_near(s):
        @pl.when(s < near)
        def _():
            b = lax.rem(s, 4)
            fetch(table[NEAR_A + jnp.minimum(s, NEAR - 1)], x_buf.at[b], sem_x.at[b])

    def near_term(z_ref, first, s):
        b = lax.rem(s, 4)
        return product(z_ref[s - first], x_buf[b])

    def near_ready(s):
        b = lax.rem(s, 4)
        fetched(x_buf.at[b], sem_x.at[b])

    def far_term(s):
        return product(v_ref[s], product(u_ref[s], fx_buf[s]))

    fetch_near(0)
    fetch_near(1)

    def far_start(s, _):
        fetch(table[FAR_A + s], fx_buf.at[s], sem_fx.at[s])
        return 0

    lax.fori_loop(0, far, far_start, 0)
    for out_ref in (*outs, token):
        out_ref[...] = jnp.zeros_like(out_ref)

    def both_step(s, _):
        fetch_near(s + 2)
        near_ready(s)
        fetched(fx_buf.at[s], sem_fx.at[s])
        near_part, far_part = near_term(za_ref, 0, s), far_term(s)
        add(table[NEAR_B + s], near_part)
        add(table[FAR_B + s], far_part)
        return 0

    def near_step(z_ref, first):
        def step(s, _):
            fetch_near(s + 2)
            near_ready(s)
            add(table[NEAR_B + s], near_term(z_ref, first, s))
            return 0

        return step

    def near_steps(z_ref, first, start, stop):
        pairs = lax.div(stop - start, 2)

        def two_steps(i, _):
            s = start + 2 * i
            fetch_near(s + 2)
            fetch_near(s + 3)
            near_ready(s)
            near_ready(s + 1)
            terms = near_term(z_ref, first, s), near_term(z_ref, first, s + 1)
            add(table[NEAR_B + s], terms[0])
            add(table[NEAR_B + s + 1], terms[1])
            return 0

        lax.fori_loop(0, pairs, two_steps, 0)
        lax.fori_loop(start + 2 * pairs, stop, near_step(z_ref, first), 0)

    together = jnp.minimum(near, far)
    lax.fori_loop(0, together, both_step, 0)
    first_stop = jnp.minimum(near, slots)
    near_steps(za_ref, 0, together, first_stop)
    near_steps(zb_ref, slots, first_stop, near)

    def far_step(s, _):
        fetched(fx_buf.at[s], sem_fx.at[s])
        add(table[FAR_B + s], far_term(s))
        return 0

    lax.fori_loop(together, far, far_step, 0)


def apply_blocks(table, held, blocks, index):
    return pl.pallas_call(
        apply_kernel,
        name=f"apply_{index}",
        in_specs=[SMEM] + [ANY] * 2 + [VMEM] * 4,
        out_specs=[VMEM] * 6,
        out_shape=[jax.ShapeDtypeStruct((n, CLUSTER // 2, WIDE), jnp.float32) for n in (4, 4, 2, 2, 4)] + [TOKEN],
        scratch_shapes=[
            pltpu.VMEM((4, CLUSTER, WIDE), jnp.float32),
            pltpu.VMEM((FAR, CLUSTER, WIDE), jnp.float32),
            pltpu.SemaphoreType.DMA((4,)),
            pltpu.SemaphoreType.DMA((FAR,)),
        ],
        compiler_params=pltpu.CompilerParams(vmem_limit_bytes=SCOPED),
        cost_estimate=pl.CostEstimate(flops=40 << 30, bytes_accessed=1, transcendentals=0),
    )(table, *held, *blocks)


def finish_kernel(*refs):
    parts, tokens, out_ref = refs[:8], refs[8:10], refs[10]
    for chunk in range(CHUNKS):
        own, *came = parts[chunk * 4 : chunk * 4 + 4]
        total = own[...] + came[0][...] + came[1][...] + came[2][...] + tokens[chunk][0, 0]
        for part in range(2):
            first = part * CHUNKS * HALF + chunk * HALF
            out_ref[:, first : first + HALF] = total[:, part * HALF : (part + 1) * HALF]


def finish(parts, tokens):
    rows = parts[0].shape[0]
    return pl.pallas_call(
        finish_kernel,
        name="finish",
        in_specs=[VMEM] * 10,
        out_specs=VMEM,
        out_shape=jax.ShapeDtypeStruct((rows, CHUNKS * WIDE), jnp.float32),
        compiler_params=pltpu.CompilerParams(vmem_limit_bytes=SCOPED),
        cost_estimate=pl.CostEstimate(flops=1 << 20, bytes_accessed=3 << 20, transcendentals=0),
    )(*parts, *tokens)


def scalars(near_pairs, far_pairs, far_ranks, block_counts):
    row_base = lax.axis_index(ROW) * 8
    col_base = lax.axis_index(COL) * 8
    core = lax.axis_index("core")
    index = lax.iota(jnp.int32, 16)
    steps_y = (index // 2 - lax.axis_index("y")) % 4
    steps_z = (index % 2 * 2 + index // 8 - lax.axis_index("zhi") * 2 - lax.axis_index("dir")) % 4
    order = jnp.where(core == 0, steps_y * 4 + steps_z, steps_z * 4 + steps_y)
    pieces = [
        block_counts[0],
        near_pairs[:, 0] - row_base,
        near_pairs[:, 1] - col_base,
        far_pairs[:, 0] - row_base,
        far_pairs[:, 1] - col_base,
        far_ranks,
        order,
        core[None],
        lax.axis_index("x")[None],
    ]
    return jnp.concatenate(pieces).astype(jnp.int32)


def shards(cotangent, radiation, near_z, near_pairs, far_ut, far_vt, far_pairs, far_ranks, block_counts):
    table = scalars(near_pairs, far_pairs, far_ranks, block_counts)
    own_0, own_1 = partial_rhs(cotangent, radiation)
    swap = [(0, 1), (1, 0)]
    first_turn, second_turn = rotations()

    def across_dir(part, name):
        with jax.named_scope(name):
            return lax.ppermute(part, "dir", swap)

    def step(part, k, name):
        with jax.named_scope(name):
            return lax.ppermute(part, "x", [(i, (i + k) % 4) for i in range(4)])

    def both_cores(parts, index):
        mine = pack(parts, index)
        with jax.named_scope(f"other_core_{index}"):
            return mine, lax.ppermute(mine, "core", swap)

    middle = CLUSTER // 2
    blocks_a, done_a = prepare_near(table, near_z, 0, NEAR // 2)
    upper, lower = own_0[:middle], own_0[middle:]
    upper = upper + (across_dir(upper, "dir_upper") + done_a[0, 0])
    blocks_b, done_b = prepare_near(table, near_z, NEAR // 2, NEAR // 2)
    upper, lower = lax.optimization_barrier((upper, lower))
    left_u, right_u = step(upper, 1, "left_upper"), step(upper, 3, "right_upper")
    lower = lower + (across_dir(lower, "dir_lower") + done_b[0, 0])
    own_1, lower, left_u, right_u = lax.optimization_barrier((own_1, lower, left_u, right_u))
    left_l, right_l = step(lower, 1, "left_lower"), step(lower, 3, "right_lower")
    came_1 = across_dir(own_1, "dir_second")
    right_l, table_far = lax.optimization_barrier((right_l, table))
    blocks_u, blocks_v, done_far = prepare_far(table_far, far_ut, far_vt)
    upper_0, lower_0 = step(left_u, 1, "pass_upper"), step(right_l, 3, "pass_lower")
    own_1 = own_1 + (came_1 + done_far[0, 0])
    own_1, upper_0, lower_0 = lax.optimization_barrier((own_1, upper_0, lower_0))
    left_1, right_1 = step(own_1, 1, "left_second"), step(own_1, 3, "right_second")
    across_1 = step(own_1, 2, "across_second")
    held_0 = both_cores([upper, lower, left_u, left_l, upper_0, lower_0, right_u, right_l], 0)
    blocks = (blocks_a, blocks_b, blocks_u, blocks_v)


    def go(part, turn, name):
        with jax.named_scope(name):
            return lax.ppermute(part, AXES, turn)

    def first_step(upper, lower, index):
        return go(upper, first_turn[0], f"ring_first_{index}"), go(lower, first_turn[2], f"ring_first_{index}")

    def second_step(ahead, behind, came, index):
        ahead, behind = ahead.at[:2].add(came[0]), behind.at[2:].add(came[1])
        return go(ahead, first_turn[0], f"ring_second_{index}"), go(behind, first_turn[2], f"ring_second_{index}")

    def other_ring(mine, came, index):
        mine, *away = [mine[k] + came[0][k] + came[1][k] for k in range(4)]
        return mine, [go(part, turn, f"other_ring_{index}") for part, turn in zip(away, second_turn)]

    mine, ahead, upper_0, lower_0, behind, done_0 = apply_blocks(table, held_0, blocks, 0)
    came_0 = first_step(upper_0, lower_0, 0)
    *parts_1, came_u, came_l, done_0 = lax.optimization_barrier((own_1, left_1, across_1, right_1, *came_0, done_0))
    came_0 = came_u, came_l
    came_0 = second_step(ahead, behind, came_0, 0)
    mine_1, ahead, upper_1, lower_1, behind, done_1 = apply_blocks(table, both_cores(parts_1, 1), blocks, 1)
    upper_1, lower_1, *came_0 = lax.optimization_barrier((upper_1, lower_1, *came_0))
    first = other_ring(mine, came_0, 0)
    came_1 = second_step(ahead, behind, first_step(upper_1, lower_1, 1), 1)
    last = other_ring(mine_1, came_1, 1)
    return finish([first[0], *first[1], last[0], *last[1]], [done_0, done_1])


def solution(mesh):
    finer = Mesh(mesh.devices.reshape(SIZES), AXES)
    blocks = P(None, AXES, None, None)
    in_specs = (
        P("dir", None),
        P(None, ("y", "zhi", "x", "core"), "dir"),
        blocks,
        P(AXES, None),
        blocks,
        blocks,
        P(AXES, None),
        P(AXES),
        P(AXES, None),
    )
    out_specs = P(("x", "core", "dir", "y", "zhi"), None)
    return jax.shard_map(shards, mesh=finer, in_specs=in_specs, out_specs=out_specs, check_vma=False)
```
